512 devices in a mesh: px: 16 (over z), py: 32 (over y, x, core).
Axes of the slice: x: 4, y: 4, z: 16, core: 2. Of those that a mesh axis runs over, the one named last changes fastest.
Arguments:
- displacement: float32 [6, 128, 4096], P(None, 'px', 'py'), may hold values from -6 to 6
- velocity: float32 [6, 128, 4096], P(None, 'px', 'py'), may hold values from -6 to 6
- external_force: float32 [6, 128, 4096], P(None, 'px', 'py')
- lumped_mass: float32 [128, 4096], P('px', 'py'), may hold values from 0.5 to 2
- thickness: float32 [128, 4096], P('px', 'py')
- added_mass: float32 [128, 4096], P('px', 'py'), may hold values from 0.5 to 4
- stiffness: float32 [24, 24], replicated, as said below
- elements: int32 [160, 4096], P('px', 'py'), may hold values from 0 to 1168, as said below
- counts: int32 [16, 32], P('px', 'py'), may hold values from 1 to 1161
Outputs:
- new_velocity: float32 [6, 128, 4096], P(None, 'px', 'py')
- new_displacement: float32 [6, 128, 4096], P(None, 'px', 'py')
The draws below stay inside these ranges and needn't reach their ends.
Inputs may be any that keep to these rules, and one draw needn't show every extreme that they name: Each partition lists every element that touches one of its nodes, lies wholly inside the grid and is live, first and in some order, then the other elements of its extended block and zeros; an element is live for all partitions that list it or for none. `stiffness`: symmetric.
All inputs are finite; a program needn't handle non-finite values.
Results may differ from the reference program's by a relative error of at most 0.0003.
Values sent between devices are 32-bit elements; how exact they have to be, the bound alone decides.
A program may use at most 64 MiB of HBM per device.

```python
import math
import jax
import jax.numpy as jnp
from jax import lax

R = 8
C = 128
ITERS = 4
TILES = 10
NR = 128
NC = 4096
N_PX = 16
N_PY = 32


def cell_lists(key):
    base = jax.random.fold_in(key, 7)
    subkeys = jax.random.split(base, 5)
    grid_rows = NR // R
    grid_cols = NC // C
    levels = jax.random.randint(subkeys[0], (grid_rows, grid_cols), 0, 4)
    pick_row = jax.random.randint(subkeys[1], (), 1, grid_rows - 1)
    pick_col = jax.random.randint(subkeys[2], (), 1, grid_cols - 1)
    row_ids = lax.broadcasted_iota(jnp.int32, (grid_rows, grid_cols), 0)
    col_ids = lax.broadcasted_iota(jnp.int32, (grid_rows, grid_cols), 1)
    dense = ((row_ids == pick_row) | (row_ids == pick_row - 1)) & ((col_ids == pick_col) | (col_ids == pick_col - 1))
    levels = jnp.where(dense, 3, levels)
    cell_levels = jnp.repeat(jnp.repeat(levels, R, axis=0), C, axis=1)
    draw_dice = jax.random.randint(subkeys[3], (NR, NC), 0, 8)
    node_rows = lax.broadcasted_iota(jnp.int32, (NR, NC), 0)
    node_cols = lax.broadcasted_iota(jnp.int32, (NR, NC), 1)
    inside = (node_rows < NR - 1) & (node_cols < NC - 1)
    alive = ((draw_dice < jnp.left_shift(1, cell_levels)) & inside).astype(jnp.int32)
    padded = jnp.pad(alive, ((1, 0), (1, 0)))

    def single(device):
        top = device // grid_cols * R
        left = device % grid_cols * C
        window = lax.dynamic_slice(padded, (top, left), (R + 1, C + 1)).reshape(-1)
        length = window.shape[0]
        shuffled = jax.random.permutation(jax.random.fold_in(subkeys[4], device), length).astype(jnp.int32)
        slots = jnp.arange(length, dtype=jnp.int32)
        scores = jnp.where(window > 0, shuffled, length + slots)
        ordering = jnp.argsort(scores, stable=True).astype(jnp.int32)
        element_ids = ordering // (C + 1) * (C + 2) + ordering % (C + 1)
        element_ids = jnp.pad(element_ids, (0, TILES * 128 - length))
        return (element_ids, jnp.sum(window).astype(jnp.int32))
    element_ids, live_counts = jax.vmap(single)(jnp.arange(grid_rows * grid_cols, dtype=jnp.int32))
    return (element_ids, live_counts.reshape(grid_rows, grid_cols), grid_rows, grid_cols)


def draw_elements(key, part):
    element_ids, live_counts, grid_rows, grid_cols = cell_lists(key)
    return element_ids.reshape(grid_rows, grid_cols, TILES, 128).transpose(0, 2, 1, 3).reshape(grid_rows * TILES, grid_cols * 128)


def draw_counts(key, part):
    element_ids, live_counts, grid_rows, grid_cols = cell_lists(key)
    return live_counts


def draw_external_force(key, part):
    node_rows = lax.broadcasted_iota(jnp.float32, (6, NR, NC), 1)
    node_cols = lax.broadcasted_iota(jnp.float32, (6, NR, NC), 2)
    ramp = 1.0 + node_rows / (NR - 1) + node_cols / (NC - 1)
    base = jnp.clip(jax.random.normal(key, (6, NR, NC), jnp.float32), -5.0, 5.0)
    return base * ramp


def draw_thickness(key, part):
    first_key, second_key = jax.random.split(jax.random.fold_in(key, 11))
    grid_rows = NR // R
    grid_cols = NC // C
    base = jnp.exp(jax.random.uniform(first_key, (NR, NC), jnp.float32, jnp.log(0.5), jnp.log(2.0)))
    factor = jnp.exp(jax.random.uniform(second_key, (grid_rows, grid_cols), jnp.float32, 0.0, jnp.log(4.0)))
    return base * jnp.repeat(jnp.repeat(factor, R, axis=0), C, axis=1)


def draw_stiffness(key, part):
    first_key, second_key = jax.random.split(jax.random.fold_in(key, 13))
    raw = jax.random.uniform(first_key, (24, 24), jnp.float32, -0.075, 0.075)
    symmetric = 0.5 * (raw + raw.T)
    diagonal = jax.random.uniform(second_key, (24,), jnp.float32, 1.8, 2.6)
    eye_mask = (lax.broadcasted_iota(jnp.int32, (24, 24), 0) == lax.broadcasted_iota(jnp.int32, (24, 24), 1)).astype(jnp.float32)
    return symmetric * (1.0 - eye_mask) + eye_mask * diagonal[None, :]


def steps_of(rng, shape, shards, smallest, top_value):
    factor_of = 1.0
    for dim, blocks in shards:
        heights = jax.random.uniform(jax.random.fold_in(jax.random.fold_in(rng, 6), dim), (blocks,), jnp.float32, smallest / len(shards), top_value / len(shards))
        factor_of = factor_of * jnp.repeat(jnp.exp(heights), shape[dim] // blocks).reshape((-1,) + (1,) * (len(shape) - 1 - dim))
    return factor_of


def gaussian(own_key, shape, scale, reach, pieces=(), kind=jnp.bfloat16):
    values = scale * jax.random.normal(own_key, shape, jnp.float32)
    if pieces:
        values = values * steps_of(own_key, shape, pieces, -0.22, 0.18)
    return jnp.clip(values, -reach, reach).astype(kind)


def setup_inputs(seed: int = 0) -> dict:
    seeds = jax.random.split(jax.random.key(seed), 10)
    return {
        "displacement": gaussian(seeds[0], (6, NR, NC), 1.0, 6.0, ((1, 16), (2, 32)), jnp.float32),
        "velocity": gaussian(seeds[1], (6, NR, NC), 1.0, 6.0, ((1, 16), (2, 32)), jnp.float32),
        "external_force": draw_external_force(jax.random.fold_in(seeds[9], 71), 0),
        "lumped_mass": jnp.clip(jnp.exp(math.log(2.0) - 1.3862944 * jax.random.uniform(seeds[3], (NR, NC), jnp.float32) ** steps_of(seeds[3], (NR, NC), ((0, 16), (1, 32)), -0.2, 0.2)), 0.5, 2.0),
        "thickness": draw_thickness(jax.random.fold_in(seeds[9], 71), 0),
        "added_mass": jnp.clip(jnp.exp(math.log(4.0) - 2.0794415 * jax.random.uniform(seeds[5], (NR, NC), jnp.float32) ** steps_of(seeds[5], (NR, NC), ((0, 16), (1, 32)), -0.2, 0.2)), 0.5, 4.0),
        "stiffness": draw_stiffness(jax.random.fold_in(seeds[9], 71), 0),
        "elements": draw_elements(jax.random.fold_in(seeds[9], 71), 0),
        "counts": draw_counts(jax.random.fold_in(seeds[9], 71), 0),
    }


highest = lax.Precision.HIGHEST

def corner_nodes(element_ids, stride):
    return jnp.stack([element_ids, element_ids + 1, element_ids + stride, element_ids + stride + 1])

def assemble(extended, element_ids, weight, kernel, stride):
    corners = corner_nodes(element_ids, stride)
    values = kernel(extended[:, corners], weight)
    summed = jnp.zeros(extended.shape, jnp.float32)
    return summed.at[:, corners.reshape(-1)].add(values.reshape(extended.shape[0], -1))

def mass_kernel(gathered, weight):
    return (gathered - lax.optimization_barrier(jnp.mean(gathered, axis=1, keepdims=True))) * weight

def diag_kernel(gathered, weight):
    return jnp.broadcast_to(0.75 * weight, gathered.shape)

def interior(extended):
    return extended.reshape(extended.shape[0], R + 2, C + 2)[:, 1:-1, 1:-1]

def reference(displacement, velocity, external_force, lumped_mass, thickness, added_mass, stiffness, elements, counts):
    stride = C + 2
    devices = N_PX * N_PY
    lists = elements.reshape(N_PX, TILES, N_PY, 128).transpose(0, 2, 1, 3).reshape(devices, TILES * 128)
    live_counts = counts.reshape(devices)
    cell_data = jnp.stack([thickness, added_mass, lumped_mass])

    def stiff_kernel(gathered, weight):
        return (jnp.dot(stiffness, gathered.reshape(24, -1), precision=highest) * weight).reshape(gathered.shape)

    def over_devices(local_fn, fields):
        padded = tuple((jnp.pad(field_in, ((0, 0), (1, 1), (1, 1))) for field_in in fields))

        def single(entry):
            device, element_ids, live_count = entry
            row_start = (device // N_PY * R).astype(jnp.int32)
            col_start = (device % N_PY * C).astype(jnp.int32)
            anchor = jnp.zeros((), jnp.int32)
            windows = tuple((lax.dynamic_slice(grid, (anchor, row_start, col_start), (grid.shape[0], R + 2, C + 2)).reshape(grid.shape[0], -1) for grid in padded))
            active = (jnp.arange(element_ids.shape[0], dtype=jnp.int32) < live_count).astype(jnp.float32)
            return local_fn(windows, element_ids, active)
        return lax.map(single, (jnp.arange(devices, dtype=jnp.int32), lists, live_counts))

    def to_grid(blocks):
        depth = blocks.shape[1]
        return blocks.reshape(N_PX, N_PY, depth, R, C).transpose(2, 0, 3, 1, 4).reshape(depth, NR, NC)

    def force_fn(windows, element_ids, active):
        extended, cells = windows
        return interior(assemble(extended, element_ids, cells[0][element_ids] * active, stiff_kernel, stride))

    def diag_fn(windows, element_ids, active):
        cells = windows[0]
        unit_field = jnp.ones((1, cells.shape[1]), jnp.float32)
        return interior(assemble(unit_field, element_ids, cells[1][element_ids] * active, diag_kernel, stride))

    def mass_fn(windows, element_ids, active):
        extended, cells = windows
        return interior(assemble(extended, element_ids, cells[1][element_ids] * active, mass_kernel, stride))

    def step_fn(windows, element_ids, active):
        cells = windows[0]
        corners = corner_nodes(element_ids, stride)
        mass_sum = lax.optimization_barrier(jnp.sum(cells[2][corners], axis=0))
        stable = 0.5 * jnp.sqrt((cells[1][element_ids] + 0.25 * mass_sum) / cells[0][element_ids])
        return jnp.min(jnp.where(active > 0, stable, 1e+30))
    internal = to_grid(over_devices(force_fn, (displacement, cell_data)))
    precond = lumped_mass[None] + to_grid(over_devices(diag_fn, (cell_data,)))
    min_step = jnp.min(over_devices(step_fn, (cell_data,)))

    def apply_mass(vector):
        return lumped_mass[None] * vector + to_grid(over_devices(mass_fn, (vector, cell_data)))
    residual = external_force - internal
    scaled = residual / precond
    direction = scaled
    gamma_now = jnp.sum(residual * scaled)
    acceleration = jnp.zeros_like(residual)
    for sweep in range(ITERS):
        applied = apply_mass(direction)
        step_length = gamma_now / jnp.sum(direction * applied)
        acceleration = acceleration + step_length * direction
        if sweep + 1 < ITERS:
            residual = residual - step_length * applied
            scaled = residual / precond
            gamma_next = jnp.sum(residual * scaled)
            direction = scaled + gamma_next / gamma_now * direction
            gamma_now = gamma_next
    new_velocity = velocity + min_step * acceleration
    new_displacement = displacement + min_step * new_velocity
    return (new_velocity, new_displacement)
```

```python
import functools

import jax
import jax.numpy as jnp
from jax import lax
from jax.experimental import pallas as pl
from jax.experimental.pallas import tpu as pltpu
from jax.sharding import PartitionSpec as P

ITERS = 4
MESH = pl.DeviceIdType.MESH
WIDE = 5
F32 = jnp.float32
BF16 = jnp.bfloat16


def quadratic(left, right, moments):
    total = None
    for i, a in enumerate(left):
        inner = None
        for j, b in enumerate(right):
            term = b * moments[i + j]
            inner = term if inner is None else inner + term
        total = a * inner if total is None else total + a * inner
    return total


def coefficients(mu):
    one = jnp.ones_like(mu[0])
    zero = jnp.zeros_like(mu[0])
    energy = [mu[k] - mu[k + 1] for k in range(7)]
    scaled, direction = [one], [one]
    gamma = mu[0]
    accel = [zero] * ITERS
    for sweep in range(ITERS):
        curvature = quadratic(direction, direction, energy)
        step = jnp.clip(gamma / curvature, 0.74, 26.0)
        for i, d in enumerate(direction):
            accel[i] = accel[i] + step * d
        if sweep + 1 < ITERS:
            applied = direction + [zero]
            for i, d in enumerate(direction):
                applied[i + 1] = applied[i + 1] - d
            grown = scaled + [zero]
            scaled = [s - step * a for s, a in zip(grown, applied)]
            gamma_next = jnp.maximum(quadratic(scaled, scaled, mu), 0.0)
            ratio = gamma_next / gamma
            direction = [s + ratio * d for s, d in zip(scaled, direction + [zero])]
            gamma = gamma_next
    return accel


def kernel(
    n_px,
    n_py,
    disp,
    vel,
    force,
    mass,
    thick,
    added,
    stiff,
    elements,
    counts,
    out_vel,
    out_disp,
    own,
    weights,
    vel_v,
    stiff_v,
    elem_v,
    count_v,
    above,
    below,
    strip_out,
    strip_left,
    strip_right,
    row_plane,
    row_line,
    got_plane,
    got_line,
    in_sem,
    halo_send,
    halo_recv,
    red_send,
    red_recv,
):
    px = lax.axis_index("px")
    py = lax.axis_index("py")
    up, down = lax.rem(px + n_px - 1, n_px), lax.rem(px + 1, n_px)
    left, right = lax.rem(py + n_py - 1, n_py), lax.rem(py + 1, n_py)

    barrier = pltpu.get_barrier_semaphore()

    def greet(a, b):
        pl.semaphore_signal(barrier, inc=1, device_id=(a, b), device_id_type=MESH)

    for a in (up, down):
        for b in (left, right):
            greet(a, b)
    for k in range(1, n_py):
        greet(px, lax.rem(py + k, n_py))
    for k in range(1, n_px):
        greet(lax.rem(px + k, n_px), py)

    loads = [
        pltpu.make_async_copy(src, dst, in_sem.at[i])
        for i, (src, dst) in enumerate(
            (
                (elements, elem_v),
                (counts, count_v),
                (thick, weights.at[0]),
                (added, weights.at[1]),
                (stiff, stiff_v),
                (disp, own.at[0:6]),
                (force, own.at[6:12]),
                (mass, own.at[12]),
                (vel, vel_v),
            )
        )
    ]
    for load in loads:
        load.start()

    row8 = lax.broadcasted_iota(jnp.int32, (8, 128), 0)
    lane8 = lax.broadcasted_iota(jnp.int32, (8, 128), 1)

    loads[0].wait()
    loads[1].wait()
    ids = elem_v[...]
    tiles = ids.shape[0]
    slot = lax.broadcasted_iota(jnp.int32, (tiles, 128), 0) * 128 + lax.broadcasted_iota(
        jnp.int32, (tiles, 128), 1
    )
    id_row = lax.shift_right_logical(ids * 4033, 19)
    id_col = ids - id_row * 130
    id_row = jnp.where(slot < count_v[...], id_row, -1)
    row_sel = lax.broadcasted_iota(jnp.int32, (8, 128), 0) + 1
    col_sel = lax.broadcasted_iota(jnp.int32, (128, 128), 0) + 1
    hot_rows, hot_cols = [], []
    for t in range(tiles):
        hot_rows.append(
            jnp.where(jnp.broadcast_to(id_row[t : t + 1], (8, 128)) == row_sel, 1.0, 0.0).astype(BF16)
        )
        hot_cols.append(
            jnp.where(jnp.broadcast_to(id_col[t : t + 1], (128, 128)) == col_sel, 1.0, 0.0).astype(BF16)
        )
    live = lax.dot_general(
        jnp.concatenate(hot_rows, axis=1),
        jnp.concatenate(hot_cols, axis=1),
        (((1,), (1,)), ((), ())),
        preferred_element_type=F32,
    )
    loads[2].wait()
    loads[3].wait()
    own[13] = weights[0] * live
    own[14] = weights[1] * live

    for i in (5, 6, 7):
        loads[i].wait()
    pack_right = jnp.zeros((8, 128), F32)
    pack_left = jnp.zeros((8, 128), F32)
    group = lax.shift_right_logical(lane8, 3)
    for f in range(15):
        field = own[f]
        pack_right = jnp.where(group == f, pltpu.roll(field, (8 * f + 8) % 128, 1), pack_right)
        pack_left = jnp.where(group == f, pltpu.roll(field, 8 * f, 1), pack_left)
    strip_out[0] = pack_right
    strip_out[1] = pack_left

    loads[4].wait()
    spread = jnp.where(
        lax.shift_right_logical(lax.broadcasted_iota(jnp.int32, (192, 24), 0), 3)
        == lax.broadcasted_iota(jnp.int32, (192, 24), 1),
        1.0,
        0.0,
    ).astype(BF16)
    same_row = (lax.broadcasted_iota(jnp.int32, (192, 192), 0) & 7) == (
        lax.broadcasted_iota(jnp.int32, (192, 192), 1) & 7
    )

    def expand(part):
        tall = jnp.dot(spread, part, preferred_element_type=F32).astype(BF16)
        full = lax.dot_general(tall, spread, (((1,), (1,)), ((), ())), preferred_element_type=F32)
        return jnp.where(same_row, full, 0.0).astype(BF16)

    stiff_all = stiff_v[...]
    stiff_hi = stiff_all.astype(BF16)
    stiff_lo = (stiff_all - stiff_hi.astype(F32)).astype(BF16)
    big_hi, big_lo = expand(stiff_hi), expand(stiff_lo)

    pl.semaphore_wait(barrier, 4 + (n_py - 1) + (n_px - 1))

    plan = (
        (own.at[:, 8 - WIDE : 8, :], above.at[:, 8 - WIDE : 8, :], down, py),
        (own.at[:, 0:WIDE, :], below.at[:, 0:WIDE, :], up, py),
        (strip_out.at[0], strip_left.at[1], px, right),
        (strip_out.at[1], strip_right.at[1], px, left),
        (strip_out.at[0], strip_left.at[0], down, right),
        (strip_out.at[1], strip_right.at[0], down, left),
        (strip_out.at[0], strip_left.at[2], up, right),
        (strip_out.at[1], strip_right.at[2], up, left),
    )
    halo = [
        pltpu.make_async_remote_copy(
            src_ref=src,
            dst_ref=dst,
            send_sem=halo_send.at[i],
            recv_sem=halo_recv.at[i],
            device_id=(a, b),
            device_id_type=MESH,
        )
        for i, (src, dst, a, b) in enumerate(plan)
    ]
    for copy in halo:
        copy.start()
    for copy in halo:
        copy.wait()

    def extend(f):
        out = []
        for i in range(3):
            if i == 0:
                main = jnp.where(row8 >= 8 - WIDE, above[f], 0.0)
            elif i == 1:
                main = own[f]
            else:
                main = jnp.where(row8 < WIDE, below[f], 0.0)
            side = jnp.where(
                lane8 >= 128 - WIDE,
                pltpu.roll(strip_left[i], (120 - 8 * f) % 128, 1),
                jnp.where(lane8 < WIDE, pltpu.roll(strip_right[i], (128 - 8 * f) % 128, 1), 0.0),
            )
            out.append(jnp.concatenate([main, side], axis=1))
        return jnp.concatenate(out, axis=0)

    def next_col(x):
        return pltpu.roll(x, x.shape[1] - 1, 1)

    def prev_col(x):
        return pltpu.roll(x, 1, 1)

    def next_row(x):
        return pltpu.roll(x, x.shape[0] - 1, 0)

    def prev_row(x):
        return pltpu.roll(x, 1, 0)

    def four_sum(x):
        half = x + next_col(x)
        return half + next_row(half)

    def to_nodes(x):
        half = x + prev_row(x)
        return half + prev_col(half)

    def six(x):
        return jnp.concatenate([x] * 6, axis=0)

    field_mass, field_thick, field_added = extend(12), extend(13), extend(14)
    weight_sum = to_nodes(field_added)
    precond = field_mass + 0.75 * weight_sum
    inverse = 1.0 / precond
    quarter = 0.25 * inverse
    quarter_weight = six(quarter * weight_sum)
    quarter6 = six(quarter)
    added6 = six(field_added)

    u00 = jnp.concatenate([extend(c) for c in range(6)], axis=0)
    u01 = next_col(u00)
    u10 = next_row(u00)
    u11 = next_row(u01)
    corners = (u00, u01, u10, u11)
    forces = [[], [], [], []]
    products = []
    for t in range(3):
        stacked = jnp.concatenate(
            [corners[n][24 * c + 8 * t : 24 * c + 8 * t + 8] for c in range(6) for n in range(4)],
            axis=0,
        )
        hi = stacked.astype(BF16)
        lo = (stacked - hi.astype(F32)).astype(BF16)
        product = (
            jnp.dot(big_hi, lo, preferred_element_type=F32)
            + jnp.dot(big_lo, hi, preferred_element_type=F32)
        ) + jnp.dot(big_hi, hi, preferred_element_type=F32)
        products.append(product)
    for n in range(4):
        forces[n] = jnp.concatenate(
            [
                products[t][8 * (4 * c + n) : 8 * (4 * c + n) + 8] * field_thick[8 * t : 8 * t + 8]
                for c in range(6)
                for t in range(3)
            ],
            axis=0,
        )
    internal = (forces[0] + prev_row(forces[2])) + prev_col(forces[1] + prev_row(forces[3]))
    external = jnp.concatenate([extend(6 + c) for c in range(6)], axis=0)
    powers = [(external - internal) * six(inverse)]
    for k in range(4):
        p = powers[-1]
        powers.append(quarter6 * to_nodes(added6 * four_sum(p)) - quarter_weight * p)

    def own_part(x):
        return [x[24 * c + 8 : 24 * c + 16, 0:128] for c in range(6)]

    mine = [own_part(x) for x in powers]
    mass_own = precond[8:16, 0:128]
    rows = []
    for k in range(8):
        a, b = mine[k // 2], mine[k - k // 2]
        total = a[0] * b[0]
        for c in range(1, 6):
            total = total + a[c] * b[c]
        rows.append(jnp.sum(total * mass_own, axis=0, keepdims=True))
    sums = jnp.sum(jnp.concatenate(rows, axis=0), axis=1, keepdims=True)
    row = jnp.sum(jnp.where(row8 == lane8, sums, 0.0), axis=0, keepdims=True)
    thick_own = own[13]
    around = four_sum(field_mass)[8:16, 0:128]
    stable = 0.5 * jnp.sqrt((weights[1] + 0.25 * around) / weights[0])
    smallest = jnp.min(jnp.where(live > 0, stable, 1e30), keepdims=True)
    lane1 = lax.broadcasted_iota(jnp.int32, (1, 128), 1)
    row = jnp.where(lane1 == 8, smallest, row)

    def gather(row, size, here, src, slots, device, i):
        src[...] = row
        slots[pl.ds(here, 1)] = row.reshape(1, 1, 128)
        for k in range(1, size):
            there = lax.rem(here + k, size)
            pltpu.make_async_remote_copy(
                src_ref=src,
                dst_ref=slots.at[here],
                send_sem=red_send.at[i],
                recv_sem=red_recv.at[i],
                device_id=device(there),
                device_id_type=MESH,
            ).start()
        most = slots.at[pl.ds(0, size - 1)]
        pltpu.make_async_copy(most, most, red_recv.at[i]).wait()
        pltpu.make_async_copy(most, most, red_send.at[i]).wait()
        sums = [slots[k] for k in range(size)]
        lows = sums
        while len(sums) > 1:
            odd = len(sums) % 2
            sums, lows = (
                [sums[j] + sums[j + 1] for j in range(0, len(sums) - odd, 2)] + sums[len(sums) - odd :],
                [jnp.minimum(lows[j], lows[j + 1]) for j in range(0, len(lows) - odd, 2)]
                + lows[len(lows) - odd :],
            )
        return jnp.where(lane1 == 8, lows[0], sums[0])

    row = gather(row, n_py, py, row_plane, got_plane, lambda there: (px, there), 0)
    row = gather(row, n_px, px, row_line, got_line, lambda there: (there, py), 1)

    accel = coefficients([row[:, k : k + 1] for k in range(8)])
    min_step = row[:, 8:9]
    loads[8].wait()
    for c in range(6):
        total = accel[0] * mine[0][c]
        for k in range(1, ITERS):
            total = total + accel[k] * mine[k][c]
        new_vel = vel_v[c] + min_step * total
        out_vel[c] = new_vel
        out_disp[c] = own[c] + min_step * new_vel


def local(n_px, n_py, *args):
    shape = args[0].shape
    tiles = args[7].shape[0]
    vmem = lambda *dims: pltpu.VMEM(dims, F32)
    return tuple(
        pl.pallas_call(
            functools.partial(kernel, n_px, n_py),
            out_shape=[jax.ShapeDtypeStruct(shape, F32)] * 2,
            in_specs=[pl.BlockSpec(memory_space=pl.ANY)] * 9,
            out_specs=[pl.BlockSpec(memory_space=pltpu.VMEM)] * 2,
            scratch_shapes=[
                vmem(15, 8, 128),
                vmem(2, 8, 128),
                vmem(6, 8, 128),
                vmem(24, 24),
                pltpu.VMEM((tiles, 128), jnp.int32),
                pltpu.VMEM((1, 1), jnp.int32),
                vmem(15, 8, 128),
                vmem(15, 8, 128),
                vmem(2, 8, 128),
                vmem(3, 8, 128),
                vmem(3, 8, 128),
                vmem(1, 128),
                vmem(1, 128),
                vmem(n_py, 1, 128),
                vmem(n_px, 1, 128),
                pltpu.SemaphoreType.DMA((9,)),
                pltpu.SemaphoreType.DMA((8,)),
                pltpu.SemaphoreType.DMA((8,)),
                pltpu.SemaphoreType.DMA((2,)),
                pltpu.SemaphoreType.DMA((2,)),
            ],
            compiler_params=pltpu.CompilerParams(collective_id=0, has_side_effects=True),
            name="crash_step",
        )(*args)
    )


def solution(mesh):
    field = P(None, "px", "py")
    plane = P("px", "py")
    return jax.shard_map(
        functools.partial(local, mesh.shape["px"], mesh.shape["py"]),
        mesh=mesh,
        in_specs=(field, field, field, plane, plane, plane, P(), plane, plane),
        out_specs=(field, field),
        check_vma=False,
    )
```

```python
import functools

import jax
import jax.numpy as jnp
from jax import lax
from jax.experimental import pallas as pl
from jax.experimental.pallas import tpu as pltpu
from jax.sharding import PartitionSpec as P

ITERS = 4
FIELDS = 15
MESH = pl.DeviceIdType.MESH
F32 = jnp.float32
BF16 = jnp.bfloat16


def quadratic(left, right, moments):
    total = None
    for i, a in enumerate(left):
        inner = None
        for j, b in enumerate(right):
            term = b * moments[i + j]
            inner = term if inner is None else inner + term
        total = a * inner if total is None else total + a * inner
    return total


def coefficients(mu):
    one = jnp.ones_like(mu[0])
    zero = jnp.zeros_like(mu[0])
    energy = [mu[k] - mu[k + 1] for k in range(7)]
    scaled, direction = [one], [one]
    gamma = mu[0]
    accel = [zero] * ITERS
    for sweep in range(ITERS):
        curvature = quadratic(direction, direction, energy)
        step = jnp.clip(gamma / curvature, 0.74, 26.0)
        for i, d in enumerate(direction):
            accel[i] = accel[i] + step * d
        if sweep + 1 < ITERS:
            applied = direction + [zero]
            for i, d in enumerate(direction):
                applied[i + 1] = applied[i + 1] - d
            scaled = [s - step * a for s, a in zip(scaled + [zero], applied)]
            gamma_next = jnp.maximum(quadratic(scaled, scaled, mu), 0.0)
            ratio = gamma_next / gamma
            direction = [s + ratio * d for s, d in zip(scaled, direction + [zero])]
            gamma = gamma_next
    return accel


def base_of(f):
    return 9 * f + 4 if f < 6 else 54 + 8 * (f - 6) + 4


def kernel(
    n_px,
    n_py,
    disp,
    force,
    mass,
    thick,
    added,
    stiff,
    elements,
    counts,
    out_gain,
    out_step,
    own,
    weights,
    stiff_v,
    elem_v,
    count_v,
    above,
    below,
    strip_out,
    strips,
    row_plane,
    row_line,
    got_plane,
    got_line,
    in_sem,
    halo_send,
    halo_recv,
    red_send,
    red_recv,
    relay,
):
    px = lax.axis_index("px")
    py = lax.axis_index("py")

    def at_px(k):
        return lax.rem(px + (n_px + k), n_px)

    def at_py(k):
        return lax.rem(py + (n_py + k), n_py)

    loads = [
        pltpu.make_async_copy(src, dst, in_sem.at[i])
        for src, dst, i in (
            (elements, elem_v, 0),
            (counts, count_v, 1),
            (thick, weights.at[0], 2),
            (added, weights.at[1], 2),
            (disp, own.at[0:6], 3),
            (force, own.at[6:12], 3),
            (mass, own.at[12], 3),
            (stiff, stiff_v, 4),
        )
    ]
    for load in loads:
        load.start()

    up, down, left, right = at_px(-1), at_px(1), at_py(-1), at_py(1)
    barrier = pltpu.get_barrier_semaphore()

    def signal(sem, a, b):
        pl.semaphore_signal(sem, inc=1, device_id=(a, b), device_id_type=MESH)

    around = [(up, left), (up, py), (up, right), (px, left), (px, right), (down, left), (down, py), (down, right)]
    for a, b in around:
        signal(barrier, a, b)

    row8 = lax.broadcasted_iota(jnp.int32, (8, 128), 0)
    lane8 = lax.broadcasted_iota(jnp.int32, (8, 128), 1)

    loads[0].wait()
    loads[1].wait()
    ids = elem_v[...]
    tiles = ids.shape[0]
    slot = lax.broadcasted_iota(jnp.int32, (tiles, 128), 0) * 128 + lax.broadcasted_iota(
        jnp.int32, (tiles, 128), 1
    )
    id_row = lax.shift_right_logical(ids * 4033, 19)
    id_col = ids - id_row * 130
    id_row = jnp.where(slot < count_v[...], id_row, -1)
    row_sel = row8 + 1
    col_sel = lax.broadcasted_iota(jnp.int32, (128, 128), 0) + 1
    hot_rows, hot_cols = [], []
    for t in range(tiles):
        hot_rows.append(
            jnp.where(jnp.broadcast_to(id_row[t : t + 1], (8, 128)) == row_sel, 1.0, 0.0).astype(BF16)
        )
        hot_cols.append(
            jnp.where(jnp.broadcast_to(id_col[t : t + 1], (128, 128)) == col_sel, 1.0, 0.0).astype(BF16)
        )
    live = lax.dot_general(
        jnp.concatenate(hot_rows, axis=1),
        jnp.concatenate(hot_cols, axis=1),
        (((1,), (1,)), ((), ())),
        preferred_element_type=F32,
    )
    pltpu.make_async_copy(weights, weights, in_sem.at[2]).wait()
    own[13] = weights[0] * live
    own[14] = weights[1] * live

    pltpu.make_async_copy(own.at[0:13], own.at[0:13], in_sem.at[3]).wait()
    lane_group = jnp.where(
        lane8 < 54, lax.shift_right_logical(lane8 * 57, 9), lax.shift_right_logical(lane8 - 54, 3) + 6
    )
    from_left = jnp.where(lane8 < 54, lane8 - 9 * lane_group, (lane8 - 54) & 7) < 4
    packed = jnp.zeros((8, 128), F32)
    for f in range(FIELDS):
        packed = jnp.where(lane_group == f, pltpu.roll(own[f], base_of(f), 1), packed)
    strip_out[...] = packed

    pl.semaphore_wait(barrier, 8)

    halo = [
        pltpu.make_async_remote_copy(
            src_ref=src,
            dst_ref=dst,
            send_sem=halo_send.at[i],
            recv_sem=halo_recv.at[i],
            device_id=(a, b),
            device_id_type=MESH,
        )
        for src, dst, a, b, i in (
            (strip_out, strips.at[2], down, right, 0),
            (strip_out, strips.at[3], down, left, 0),
            (strip_out, strips.at[4], up, right, 0),
            (strip_out, strips.at[5], up, left, 0),
            (strip_out, strips.at[0], px, right, 0),
            (strip_out, strips.at[1], px, left, 0),
            (own.at[:, 4:8, :], above.at[:, 4:8, :], down, py, 1),
            (own.at[:, 0:5, :], below.at[:, 0:5, :], up, py, 2),
        )
    ]
    for copy in halo:
        copy.start()

    def tell(k, axes):
        far = 1 << k
        if "px" in axes:
            signal(relay.at[k], at_px(far), py)
            signal(relay.at[k], at_px(-far), py)
        if "py" in axes:
            signal(relay.at[k], px, at_py(far))
            signal(relay.at[k], px, at_py(-far))

    rounds = []
    far = 1
    while 2 * far <= max(n_px, n_py) // 2:
        rounds.append([n for n, size in (("px", n_px), ("py", n_py)) if 2 * far <= size // 2])
        far *= 2

    def listen(k):
        pl.semaphore_wait(relay.at[k], 2 * len(rounds[k]))

    def relay_step(k):
        if 1 <= k <= len(rounds):
            listen(k - 1)
        if k < len(rounds):
            tell(k, rounds[k])

    relay_step(0)

    loads[7].wait()
    spread = jnp.where(
        lax.shift_right_logical(lax.broadcasted_iota(jnp.int32, (192, 24), 0), 3)
        == lax.broadcasted_iota(jnp.int32, (192, 24), 1),
        1.0,
        0.0,
    ).astype(BF16)
    same_row = (lax.broadcasted_iota(jnp.int32, (192, 192), 0) & 7) == (
        lax.broadcasted_iota(jnp.int32, (192, 192), 1) & 7
    )

    def expand(part):
        tall = jnp.dot(spread, part, preferred_element_type=F32).astype(BF16)
        full = lax.dot_general(tall, spread, (((1,), (1,)), ((), ())), preferred_element_type=F32)
        return jnp.where(same_row, full, 0.0).astype(BF16)

    stiff_all = stiff_v[...]
    stiff_hi = stiff_all.astype(BF16)
    stiff_lo = (stiff_all - stiff_hi.astype(F32)).astype(BF16)
    big_hi, big_lo = expand(stiff_hi), expand(stiff_lo)

    relay_step(1)
    relay_step(2)

    pltpu.make_async_copy(strips, strips, halo_recv.at[0]).wait()
    halo[6].wait_recv()
    halo[7].wait_recv()

    lower = row8 < 4
    side_mid = jnp.where(from_left, strips[0], strips[1])
    side_above = jnp.where(from_left, strips[2], strips[3])
    side_below = jnp.where(from_left, strips[4], strips[5])
    side_edge = jnp.where(lower, side_below, side_above)
    side_next = pltpu.roll(side_below, 7, 0)

    def unpack(tile, f):
        return pltpu.roll(tile, 128 - base_of(f), 1)

    def extend(first, count):
        fields = range(first, first + count)
        return [
            [own[first : first + count], jnp.stack([unpack(side_mid, f) for f in fields])],
            [
                jnp.where(
                    lax.broadcasted_iota(jnp.int32, (count, 8, 128), 1) < 4,
                    below[first : first + count],
                    above[first : first + count],
                ),
                jnp.stack([unpack(side_edge, f) for f in fields]),
            ],
        ]

    def each(f, *xs):
        return [[f(*[x[t][s] for x in xs]) for s in range(2)] for t in range(2)]

    def shift_rows(x, to, edge):
        r = each(lambda q: pltpu.roll(q, to % 8, 1), x)
        at = lax.broadcasted_iota(jnp.int32, x[0][0].shape, 1) == edge
        return [[jnp.where(at, r[1 - t][s], r[t][s]) for s in range(2)] for t in range(2)]

    def shift_cols(x, to, edge):
        r = each(lambda q: pltpu.roll(q, to % 128, 2), x)
        at = lax.broadcasted_iota(jnp.int32, x[0][0].shape, 2) == edge
        return [[jnp.where(at, r[t][1 - s], r[t][s]) for s in range(2)] for t in range(2)]

    def next_row(x):
        return shift_rows(x, -1, 7)

    def prev_row(x):
        return shift_rows(x, 1, 0)

    def next_col(x):
        return shift_cols(x, -1, 127)

    def prev_col(x):
        return shift_cols(x, 1, 0)

    def add(a, b):
        return each(lambda p, q: p + q, a, b)

    def four_sum(x):
        half = add(x, next_col(x))
        return add(half, next_row(half))

    def to_nodes(x):
        half = add(x, prev_row(x))
        return add(half, prev_col(half))

    u00 = extend(0, 6)
    u01 = next_col(u00)
    u10 = next_row(u00)
    at_three = lax.broadcasted_iota(jnp.int32, (6, 8, 128), 1) == 3
    u10[1] = [
        jnp.where(at_three, pltpu.roll(below[0:6], 7, 1), u10[1][0]),
        jnp.where(at_three, jnp.stack([unpack(side_next, f) for f in range(6)]), u10[1][1]),
    ]
    u11 = next_col(u10)
    corners = (u00, u01, u10, u11)
    field_mass, field_thick, field_added = extend(12, 1), extend(13, 1), extend(14, 1)
    forces = [[[None, None], [None, None]] for _ in range(4)]
    for t in range(2):
        stacked = jnp.concatenate(
            [
                jnp.concatenate([corners[n][t][s][c] for c in range(6) for n in range(4)], axis=0)
                for s in range(2)
            ],
            axis=1,
        )
        hi = stacked.astype(BF16)
        lo = (stacked - hi.astype(F32)).astype(BF16)
        product = (
            jnp.dot(big_hi, lo, preferred_element_type=F32)
            + jnp.dot(big_lo, hi, preferred_element_type=F32)
        ) + jnp.dot(big_hi, hi, preferred_element_type=F32)
        for n in range(4):
            for s in range(2):
                forces[n][t][s] = (
                    jnp.stack(
                        [
                            product[8 * (4 * c + n) : 8 * (4 * c + n) + 8, 128 * s : 128 * s + 128]
                            for c in range(6)
                        ]
                    )
                    * field_thick[t][s]
                )
    relay_step(3)
    internal = add(
        add(forces[0], prev_row(forces[2])), prev_col(add(forces[1], prev_row(forces[3])))
    )

    weight_sum = to_nodes(field_added)
    precond = each(lambda m, w: m + 0.75 * w, field_mass, weight_sum)
    inverse = each(lambda m: 1.0 / m, precond)
    quarter = each(lambda i: 0.25 * i, inverse)
    quarter_weight = each(lambda q, w: q * w, quarter, weight_sum)
    powers = [each(lambda f, g, i: (f - g) * i, extend(6, 6), internal, inverse)]
    for k in range(3):
        p = powers[-1]
        spread_sum = to_nodes(each(lambda a, s: a * s, field_added, four_sum(p)))
        powers.append(
            each(lambda q, n, w, v: q * n - w * v, quarter, spread_sum, quarter_weight, p)
        )

    mine = [x[0][0] for x in powers]
    weighted = [precond[0][0] * x for x in mine]
    moments = [jnp.sum(weighted[k // 2] * mine[k - k // 2], axis=0) for k in range(7)]
    last = four_sum(powers[3])[0][0]
    moments.append(
        0.25
        * jnp.sum(
            field_added[0][0] * (last * last) - weight_sum[0][0] * (mine[3] * mine[3]), axis=0
        )
    )
    sums = jnp.concatenate([jnp.sum(m, axis=0, keepdims=True) for m in moments], axis=0)
    sums = jnp.sum(sums, axis=1, keepdims=True)
    row = jnp.sum(jnp.where(row8 == lane8, sums, 0.0), axis=0, keepdims=True)

    around_mass = four_sum(field_mass)[0][0][0]
    stable = 0.5 * jnp.sqrt((weights[1] + 0.25 * around_mass) / weights[0])
    smallest = jnp.min(jnp.where(live > 0, stable, 1e30), keepdims=True)
    lane1 = lax.broadcasted_iota(jnp.int32, (1, 128), 1)
    row = jnp.where(lane1 == 8, smallest, row)

    for k in range(4, len(rounds) + 1):
        relay_step(k)

    def gather(row, size, here, src, slots, device, i):
        src[...] = row
        slots[pl.ds(here, 1)] = row.reshape(1, 1, 128)
        for k in range(1, size):
            pltpu.make_async_remote_copy(
                src_ref=src,
                dst_ref=slots.at[here],
                send_sem=red_send.at[i],
                recv_sem=red_recv.at[i],
                device_id=device(k),
                device_id_type=MESH,
            ).start()
        most = slots.at[pl.ds(0, size - 1)]
        pltpu.make_async_copy(most, most, red_recv.at[i]).wait()
        sums = [slots[k] for k in range(size)]
        lows = sums
        while len(sums) > 1:
            odd = len(sums) % 2
            sums, lows = (
                [sums[j] + sums[j + 1] for j in range(0, len(sums) - odd, 2)] + sums[len(sums) - odd :],
                [jnp.minimum(lows[j], lows[j + 1]) for j in range(0, len(lows) - odd, 2)]
                + lows[len(lows) - odd :],
            )
        return jnp.where(lane1 == 8, lows[0], sums[0])

    row = gather(row, n_py, py, row_plane, got_plane, lambda k: (px, at_py(k)), 0)
    row = gather(row, n_px, px, row_line, got_line, lambda k: (at_px(k), py), 1)

    row = jnp.broadcast_to(row, (8, 128))
    splat = [jnp.broadcast_to(row[:, k : k + 1], (8, 128)) for k in range(9)]
    accel = coefficients(splat[:8])
    min_step = splat[8]
    total = accel[0] * mine[0]
    for k in range(1, ITERS):
        total = total + accel[k] * mine[k]
    out_gain[...] = min_step * total
    out_step[...] = min_step

    pltpu.make_async_copy(strips, strips, halo_send.at[0]).wait()
    halo[6].wait_send()
    halo[7].wait_send()
    for i, (slots, size) in enumerate(((got_plane, n_py), (got_line, n_px))):
        most = slots.at[pl.ds(0, size - 1)]
        pltpu.make_async_copy(most, most, red_send.at[i]).wait()


def local(n_px, n_py, disp, vel, force, mass, thick, added, stiff, elements, counts):
    tiles = elements.shape[0]
    vmem = lambda *dims: pltpu.VMEM(dims, F32)
    dma = lambda n: pltpu.SemaphoreType.DMA((n,))
    gain, step = pl.pallas_call(
        functools.partial(kernel, n_px, n_py),
        out_shape=[jax.ShapeDtypeStruct(disp.shape, F32), jax.ShapeDtypeStruct((8, 128), F32)],
        in_specs=[pl.BlockSpec(memory_space=pltpu.HBM)] * 8,
        out_specs=[pl.BlockSpec(memory_space=pltpu.VMEM)] * 2,
        scratch_shapes=[
            vmem(FIELDS, 8, 128),
            vmem(2, 8, 128),
            vmem(24, 24),
            pltpu.VMEM((tiles, 128), jnp.int32),
            pltpu.VMEM((1, 1), jnp.int32),
            vmem(FIELDS, 8, 128),
            vmem(FIELDS, 8, 128),
            vmem(8, 128),
            vmem(6, 8, 128),
            vmem(1, 128),
            vmem(1, 128),
            vmem(n_py, 1, 128),
            vmem(n_px, 1, 128),
            dma(5),
            dma(3),
            dma(3),
            dma(2),
            dma(2),
            pltpu.SemaphoreType.REGULAR((4,)),
        ],
        compiler_params=pltpu.CompilerParams(collective_id=0, has_side_effects=True),
        name="crash_step",
    )(disp, force, mass, thick, added, stiff, elements, counts)
    new_velocity = vel + gain
    new_displacement = disp + step * new_velocity
    return new_velocity, new_displacement


def solution(mesh):
    field = P(None, "px", "py")
    plane = P("px", "py")
    return jax.shard_map(
        functools.partial(local, mesh.shape["px"], mesh.shape["py"]),
        mesh=mesh,
        in_specs=(field, field, field, plane, plane, plane, P(), plane, plane),
        out_specs=(field, field),
        check_vma=False,
    )
```

```python
import functools

import jax
import jax.numpy as jnp
from jax import lax
from jax.experimental import pallas as pl
from jax.experimental.pallas import tpu as pltpu
from jax.sharding import PartitionSpec as P

ITERS = 4
FIELDS = 15
MESH = pl.DeviceIdType.MESH
F32 = jnp.float32
BF16 = jnp.bfloat16


def quadratic(left, right, moments):
    total = None
    for i, a in enumerate(left):
        inner = None
        for j, b in enumerate(right):
            term = b * moments[i + j]
            inner = term if inner is None else inner + term
        total = a * inner if total is None else total + a * inner
    return total


def coefficients(mu):
    one = jnp.ones_like(mu[0])
    zero = jnp.zeros_like(mu[0])
    energy = [mu[k] - mu[k + 1] for k in range(7)]
    scaled, direction = [one], [one]
    gamma = mu[0]
    accel = [zero] * ITERS
    for sweep in range(ITERS):
        curvature = quadratic(direction, direction, energy)
        step = jnp.clip(gamma / curvature, 0.74, 26.0)
        for i, d in enumerate(direction):
            accel[i] = accel[i] + step * d
        if sweep + 1 < ITERS:
            applied = direction + [zero]
            for i, d in enumerate(direction):
                applied[i + 1] = applied[i + 1] - d
            scaled = [s - step * a for s, a in zip(scaled + [zero], applied)]
            gamma_next = jnp.maximum(quadratic(scaled, scaled, mu), 0.0)
            ratio = gamma_next / gamma
            direction = [s + ratio * d for s, d in zip(scaled, direction + [zero])]
            gamma = gamma_next
    return accel


def base_of(f):
    return 9 * f + 4 if f < 6 else 54 + 8 * (f - 6) + 4


def kernel(
    n_px,
    n_py,
    disp,
    force,
    mass,
    thick,
    added,
    stiff,
    elements,
    counts,
    out_gain,
    out_step,
    own,
    weights,
    stiff_v,
    elem_v,
    count_v,
    above,
    below,
    strip_out,
    strips,
    row_plane,
    row_line,
    got_plane,
    got_line,
    in_sem,
    halo_send,
    halo_recv,
    red_send,
    red_recv,
    relay,
):
    px = lax.axis_index("px")
    py = lax.axis_index("py")

    def at_px(k):
        return lax.rem(px + (n_px + k), n_px)

    def at_py(k):
        return lax.rem(py + (n_py + k), n_py)

    loads = [
        pltpu.make_async_copy(src, dst, in_sem.at[i])
        for src, dst, i in (
            (elements, elem_v, 0),
            (counts, count_v, 1),
            (thick, weights.at[0], 2),
            (added, weights.at[1], 2),
            (disp, own.at[0:6], 3),
            (force, own.at[6:12], 3),
            (mass, own.at[12], 3),
            (stiff, stiff_v, 4),
        )
    ]
    for load in loads:
        load.start()

    up, down, left, right = at_px(-1), at_px(1), at_py(-1), at_py(1)
    barrier = pltpu.get_barrier_semaphore()

    def signal(sem, a, b):
        pl.semaphore_signal(sem, inc=1, device_id=(a, b), device_id_type=MESH)

    span = n_py // 4 if n_py >= 8 else n_py
    start = lax.div(py, span) * span
    row_peers = [start + lax.rem(py - start + k, span) for k in range(1, span)]
    column_peers = [at_py(k) for k in range(span, n_py, span)]
    for a in (up, down):
        for b in (left, right, py):
            signal(barrier, a, b)
    for b in [left, right] + column_peers + row_peers:
        signal(barrier, px, b)

    row8 = lax.broadcasted_iota(jnp.int32, (8, 128), 0)
    lane8 = lax.broadcasted_iota(jnp.int32, (8, 128), 1)

    loads[0].wait()
    loads[1].wait()
    ids = elem_v[...]
    tiles = ids.shape[0]
    slot = lax.broadcasted_iota(jnp.int32, (tiles, 128), 0) * 128 + lax.broadcasted_iota(
        jnp.int32, (tiles, 128), 1
    )
    id_row = lax.shift_right_logical(ids * 4033, 19)
    id_col = ids - id_row * 130
    id_row = jnp.where(slot < count_v[...], id_row, -1)
    row_sel = row8 + 1
    col_sel = lax.broadcasted_iota(jnp.int32, (128, 128), 0) + 1
    hot_rows, hot_cols = [], []
    for t in range(tiles):
        hot_rows.append(
            jnp.where(jnp.broadcast_to(id_row[t : t + 1], (8, 128)) == row_sel, 1.0, 0.0).astype(BF16)
        )
        hot_cols.append(
            jnp.where(jnp.broadcast_to(id_col[t : t + 1], (128, 128)) == col_sel, 1.0, 0.0).astype(BF16)
        )
    live = lax.dot_general(
        jnp.concatenate(hot_rows, axis=1),
        jnp.concatenate(hot_cols, axis=1),
        (((1,), (1,)), ((), ())),
        preferred_element_type=F32,
    )
    pltpu.make_async_copy(weights, weights, in_sem.at[2]).wait()
    own[13] = weights[0] * live
    own[14] = weights[1] * live

    pltpu.make_async_copy(own.at[0:13], own.at[0:13], in_sem.at[3]).wait()
    lane_group = jnp.where(
        lane8 < 54, lax.shift_right_logical(lane8 * 57, 9), lax.shift_right_logical(lane8 - 54, 3) + 6
    )
    from_left = jnp.where(lane8 < 54, lane8 - 9 * lane_group, (lane8 - 54) & 7) < 4
    packed = jnp.zeros((8, 128), F32)
    for f in range(FIELDS):
        packed = jnp.where(lane_group == f, pltpu.roll(own[f], base_of(f), 1), packed)
    strip_out[...] = packed

    pl.semaphore_wait(barrier, 8 + len(row_peers) + len(column_peers))

    halo = [
        pltpu.make_async_remote_copy(
            src_ref=src,
            dst_ref=dst,
            send_sem=halo_send.at[i],
            recv_sem=halo_recv.at[i],
            device_id=(a, b),
            device_id_type=MESH,
        )
        for src, dst, a, b, i in (
            (strip_out, strips.at[2], down, right, 0),
            (strip_out, strips.at[3], down, left, 0),
            (strip_out, strips.at[4], up, right, 0),
            (strip_out, strips.at[5], up, left, 0),
            (strip_out, strips.at[0], px, right, 0),
            (strip_out, strips.at[1], px, left, 0),
            (own.at[:, 4:8, :], above.at[:, 4:8, :], down, py, 1),
            (own.at[:, 0:5, :], below.at[:, 0:5, :], up, py, 2),
        )
    ]
    for copy in halo:
        copy.start()

    for b in column_peers:
        signal(relay.at[0], px, b)
    rounds = 0
    while 2 << rounds <= n_px // 2:
        rounds += 1

    def pass_on(k):
        if 1 <= k <= rounds:
            pl.semaphore_wait(relay.at[k], 2)
        if k < rounds:
            signal(relay.at[k + 1], at_px(1 << k), py)
            signal(relay.at[k + 1], at_px(-(1 << k)), py)

    pass_on(0)

    loads[7].wait()
    spread = jnp.where(
        lax.shift_right_logical(lax.broadcasted_iota(jnp.int32, (192, 24), 0), 3)
        == lax.broadcasted_iota(jnp.int32, (192, 24), 1),
        1.0,
        0.0,
    ).astype(BF16)
    same_row = (lax.broadcasted_iota(jnp.int32, (192, 192), 0) & 7) == (
        lax.broadcasted_iota(jnp.int32, (192, 192), 1) & 7
    )

    def expand(part):
        tall = jnp.dot(spread, part, preferred_element_type=F32).astype(BF16)
        full = lax.dot_general(tall, spread, (((1,), (1,)), ((), ())), preferred_element_type=F32)
        return jnp.where(same_row, full, 0.0).astype(BF16)

    stiff_all = stiff_v[...]
    stiff_hi = stiff_all.astype(BF16)
    stiff_lo = (stiff_all - stiff_hi.astype(F32)).astype(BF16)
    big_hi, big_lo = expand(stiff_hi), expand(stiff_lo)

    pass_on(1)

    pltpu.make_async_copy(strips, strips, halo_recv.at[0]).wait()
    halo[6].wait_recv()
    halo[7].wait_recv()

    lower = row8 < 4
    side_mid = jnp.where(from_left, strips[0], strips[1])
    side_above = jnp.where(from_left, strips[2], strips[3])
    side_below = jnp.where(from_left, strips[4], strips[5])
    side_edge = jnp.where(lower, side_below, side_above)
    side_next = pltpu.roll(side_below, 7, 0)

    def unpack(tile, f):
        return pltpu.roll(tile, 128 - base_of(f), 1)

    def extend(first, count):
        fields = range(first, first + count)
        return [
            [own[first : first + count], jnp.stack([unpack(side_mid, f) for f in fields])],
            [
                jnp.where(
                    lax.broadcasted_iota(jnp.int32, (count, 8, 128), 1) < 4,
                    below[first : first + count],
                    above[first : first + count],
                ),
                jnp.stack([unpack(side_edge, f) for f in fields]),
            ],
        ]

    def each(f, *xs):
        return [[f(*[x[t][s] for x in xs]) for s in range(2)] for t in range(2)]

    def shift_rows(x, to, edge):
        r = each(lambda q: pltpu.roll(q, to % 8, 1), x)
        at = lax.broadcasted_iota(jnp.int32, x[0][0].shape, 1) == edge
        return [[jnp.where(at, r[1 - t][s], r[t][s]) for s in range(2)] for t in range(2)]

    def shift_cols(x, to, edge):
        r = each(lambda q: pltpu.roll(q, to % 128, 2), x)
        at = lax.broadcasted_iota(jnp.int32, x[0][0].shape, 2) == edge
        return [[jnp.where(at, r[t][1 - s], r[t][s]) for s in range(2)] for t in range(2)]

    def next_row(x):
        return shift_rows(x, -1, 7)

    def prev_row(x):
        return shift_rows(x, 1, 0)

    def next_col(x):
        return shift_cols(x, -1, 127)

    def prev_col(x):
        return shift_cols(x, 1, 0)

    def add(a, b):
        return each(lambda p, q: p + q, a, b)

    def four_sum(x):
        half = add(x, next_col(x))
        return add(half, next_row(half))

    def to_nodes(x):
        half = add(x, prev_row(x))
        return add(half, prev_col(half))

    u00 = extend(0, 6)
    u01 = next_col(u00)
    u10 = next_row(u00)
    at_three = lax.broadcasted_iota(jnp.int32, (6, 8, 128), 1) == 3
    u10[1] = [
        jnp.where(at_three, pltpu.roll(below[0:6], 7, 1), u10[1][0]),
        jnp.where(at_three, jnp.stack([unpack(side_next, f) for f in range(6)]), u10[1][1]),
    ]
    u11 = next_col(u10)
    corners = (u00, u01, u10, u11)
    field_mass, field_thick, field_added = extend(12, 1), extend(13, 1), extend(14, 1)
    forces = [[[None, None], [None, None]] for _ in range(4)]
    for t in range(2):
        stacked = jnp.concatenate(
            [
                jnp.concatenate([corners[n][t][s][c] for c in range(6) for n in range(4)], axis=0)
                for s in range(2)
            ],
            axis=1,
        )
        hi = stacked.astype(BF16)
        lo = (stacked - hi.astype(F32)).astype(BF16)
        product = (
            jnp.dot(big_hi, lo, preferred_element_type=F32)
            + jnp.dot(big_lo, hi, preferred_element_type=F32)
        ) + jnp.dot(big_hi, hi, preferred_element_type=F32)
        for n in range(4):
            for s in range(2):
                forces[n][t][s] = (
                    jnp.stack(
                        [
                            product[8 * (4 * c + n) : 8 * (4 * c + n) + 8, 128 * s : 128 * s + 128]
                            for c in range(6)
                        ]
                    )
                    * field_thick[t][s]
                )
    pass_on(2)
    internal = add(
        add(forces[0], prev_row(forces[2])), prev_col(add(forces[1], prev_row(forces[3])))
    )

    weight_sum = to_nodes(field_added)
    precond = each(lambda m, w: m + 0.75 * w, field_mass, weight_sum)
    inverse = each(lambda m: 1.0 / m, precond)
    quarter = each(lambda i: 0.25 * i, inverse)
    quarter_weight = each(lambda q, w: q * w, quarter, weight_sum)
    powers = [each(lambda f, g, i: (f - g) * i, extend(6, 6), internal, inverse)]
    for k in range(3):
        p = powers[-1]
        spread_sum = to_nodes(each(lambda a, s: a * s, field_added, four_sum(p)))
        powers.append(
            each(lambda q, n, w, v: q * n - w * v, quarter, spread_sum, quarter_weight, p)
        )

    mine = [x[0][0] for x in powers]
    weighted = [precond[0][0] * x for x in mine]
    moments = [jnp.sum(weighted[k // 2] * mine[k - k // 2], axis=0) for k in range(7)]
    last = four_sum(powers[3])[0][0]
    moments.append(
        0.25
        * jnp.sum(
            field_added[0][0] * (last * last) - weight_sum[0][0] * (mine[3] * mine[3]), axis=0
        )
    )
    sums = jnp.concatenate([jnp.sum(m, axis=0, keepdims=True) for m in moments], axis=0)
    sums = jnp.sum(sums, axis=1, keepdims=True)
    row = jnp.sum(jnp.where(row8 == lane8, sums, 0.0), axis=0, keepdims=True)

    around_mass = four_sum(field_mass)[0][0][0]
    stable = 0.5 * jnp.sqrt((weights[1] + 0.25 * around_mass) / weights[0])
    smallest = jnp.min(jnp.where(live > 0, stable, 1e30), keepdims=True)
    lane1 = lax.broadcasted_iota(jnp.int32, (1, 128), 1)
    row = jnp.where(lane1 == 8, smallest, row)

    if column_peers:
        pl.semaphore_wait(relay.at[0], len(column_peers))

    def gather(row, size, here, src, slots, device, far, i):
        src[...] = row
        slots[pl.ds(here, 1)] = row.reshape(1, 1, 128)
        for k in sorted(range(1, size), key=far):
            pltpu.make_async_remote_copy(
                src_ref=src,
                dst_ref=slots.at[here],
                send_sem=red_send.at[i],
                recv_sem=red_recv.at[i],
                device_id=device(k),
                device_id_type=MESH,
            ).start()
        most = slots.at[pl.ds(0, size - 1)]
        pltpu.make_async_copy(most, most, red_recv.at[i]).wait()
        sums = [slots[k] for k in range(size)]
        lows = sums
        while len(sums) > 1:
            odd = len(sums) % 2
            sums, lows = (
                [sums[j] + sums[j + 1] for j in range(0, len(sums) - odd, 2)] + sums[len(sums) - odd :],
                [jnp.minimum(lows[j], lows[j + 1]) for j in range(0, len(lows) - odd, 2)]
                + lows[len(lows) - odd :],
            )
        return jnp.where(lane1 == 8, lows[0], sums[0])

    def line_far(k):
        return -min(k, n_px - k)

    def plane_far(k):
        x, y = k // 2 % 4, k // 8
        return -(min(x, 4 - x) + min(y, 4 - y))

    row = gather(row, n_py, py, row_plane, got_plane, lambda k: (px, at_py(k)), plane_far, 0)
    for k in range(3, rounds + 1):
        pass_on(k)
    row = gather(row, n_px, px, row_line, got_line, lambda k: (at_px(k), py), line_far, 1)

    row = jnp.broadcast_to(row, (8, 128))
    splat = [jnp.broadcast_to(row[:, k : k + 1], (8, 128)) for k in range(9)]
    accel = coefficients(splat[:8])
    min_step = splat[8]
    total = accel[0] * mine[0]
    for k in range(1, ITERS):
        total = total + accel[k] * mine[k]
    out_gain[...] = min_step * total
    out_step[...] = min_step

    pltpu.make_async_copy(strips, strips, halo_send.at[0]).wait()
    halo[6].wait_send()
    halo[7].wait_send()
    for i, (slots, size) in enumerate(((got_plane, n_py), (got_line, n_px))):
        most = slots.at[pl.ds(0, size - 1)]
        pltpu.make_async_copy(most, most, red_send.at[i]).wait()


def local(n_px, n_py, disp, vel, force, mass, thick, added, stiff, elements, counts):
    tiles = elements.shape[0]
    vmem = lambda *dims: pltpu.VMEM(dims, F32)
    dma = lambda n: pltpu.SemaphoreType.DMA((n,))
    gain, step = pl.pallas_call(
        functools.partial(kernel, n_px, n_py),
        out_shape=[jax.ShapeDtypeStruct(disp.shape, F32), jax.ShapeDtypeStruct((8, 128), F32)],
        in_specs=[pl.BlockSpec(memory_space=pltpu.HBM)] * 8,
        out_specs=[pl.BlockSpec(memory_space=pltpu.VMEM)] * 2,
        scratch_shapes=[
            vmem(FIELDS, 8, 128),
            vmem(2, 8, 128),
            vmem(24, 24),
            pltpu.VMEM((tiles, 128), jnp.int32),
            pltpu.VMEM((1, 1), jnp.int32),
            vmem(FIELDS, 8, 128),
            vmem(FIELDS, 8, 128),
            vmem(8, 128),
            vmem(6, 8, 128),
            vmem(1, 128),
            vmem(1, 128),
            vmem(n_py, 1, 128),
            vmem(n_px, 1, 128),
            dma(5),
            dma(3),
            dma(3),
            dma(2),
            dma(2),
            pltpu.SemaphoreType.REGULAR((4,)),
        ],
        compiler_params=pltpu.CompilerParams(
            collective_id=0, has_side_effects=True, vmem_limit_bytes=8 << 20
        ),
        name="crash_step",
    )(*(pltpu.with_memory_space_constraint(x, pltpu.HBM) for x in (disp, force, mass, thick, added, stiff, elements)), counts)
    new_velocity = vel + gain
    new_displacement = disp + step * new_velocity
    return new_velocity, new_displacement


def solution(mesh):
    field = P(None, "px", "py")
    plane = P("px", "py")
    return jax.shard_map(
        functools.partial(local, mesh.shape["px"], mesh.shape["py"]),
        mesh=mesh,
        in_specs=(field, field, field, plane, plane, plane, P(), plane, plane),
        out_specs=(field, field),
        check_vma=False,
    )
```

```python
import functools

import jax
import jax.numpy as jnp
from jax import lax
from jax.experimental import pallas as pl
from jax.experimental.pallas import tpu as pltpu
from jax.sharding import PartitionSpec as P

ITERS = 4
FIELDS = 15
MESH = pl.DeviceIdType.MESH
F32 = jnp.float32
BF16 = jnp.bfloat16


def quadratic(left, right, moments):
    total = None
    for i, a in enumerate(left):
        inner = None
        for j, b in enumerate(right):
            term = b * moments[i + j]
            inner = term if inner is None else inner + term
        total = a * inner if total is None else total + a * inner
    return total


def coefficients(mu):
    one = jnp.ones_like(mu[0])
    zero = jnp.zeros_like(mu[0])
    energy = [mu[k] - mu[k + 1] for k in range(7)]
    scaled, direction = [one], [one]
    gamma = mu[0]
    accel = [zero] * ITERS
    for sweep in range(ITERS):
        curvature = quadratic(direction, direction, energy)
        step = jnp.clip(gamma / curvature, 0.74, 26.0)
        for i, d in enumerate(direction):
            accel[i] = accel[i] + step * d
        if sweep + 1 < ITERS:
            applied = direction + [zero]
            for i, d in enumerate(direction):
                applied[i + 1] = applied[i + 1] - d
            scaled = [s - step * a for s, a in zip(scaled + [zero], applied)]
            gamma_next = jnp.maximum(quadratic(scaled, scaled, mu), 0.0)
            ratio = gamma_next / gamma
            direction = [s + ratio * d for s, d in zip(scaled, direction + [zero])]
            gamma = gamma_next
    return accel


def base_of(f):
    return 9 * f + 4 if f < 6 else 54 + 8 * (f - 6) + 4


def kernel(
    n_px,
    n_py,
    disp,
    force,
    mass,
    thick,
    added,
    stiff,
    elements,
    counts,
    out_gain,
    out_step,
    own,
    weights,
    stiff_v,
    elem_v,
    above,
    below,
    strip_out,
    strips,
    row_plane,
    row_line,
    got_plane,
    got_line,
    in_sem,
    halo_send,
    halo_recv,
    red_send,
    red_recv,
    relay,
):
    px = lax.axis_index("px")
    py = lax.axis_index("py")

    def at_px(k):
        return lax.rem(px + (n_px + k), n_px)

    def at_py(k):
        return lax.rem(py + (n_py + k), n_py)

    loads = [
        pltpu.make_async_copy(src, dst, in_sem.at[i])
        for src, dst, i in (
            (elements, elem_v, 0),
            (thick, weights.at[0], 1),
            (added, weights.at[1], 1),
            (disp, own.at[0:6], 2),
            (force, own.at[6:12], 2),
            (mass, own.at[12], 2),
            (stiff, stiff_v, 3),
        )
    ]
    for load in loads:
        load.start()

    up, down, left, right = at_px(-1), at_px(1), at_py(-1), at_py(1)
    barrier = pltpu.get_barrier_semaphore()

    def signal(sem, a, b):
        pl.semaphore_signal(sem, inc=1, device_id=(a, b), device_id_type=MESH)

    span = n_py // 4 if n_py >= 8 else n_py
    start = lax.div(py, span) * span
    row_peers = [start + lax.rem(py - start + k, span) for k in range(1, span)]
    column_peers = [at_py(k) for k in range(span, n_py, span)]
    for a in (up, down):
        signal(barrier, a, py)
    for b in [left, right] + column_peers + row_peers:
        signal(barrier, px, b)

    row8 = lax.broadcasted_iota(jnp.int32, (8, 128), 0)
    lane8 = lax.broadcasted_iota(jnp.int32, (8, 128), 1)

    loads[0].wait()
    ids = elem_v[...]
    tiles = ids.shape[0]
    slot = lax.broadcasted_iota(jnp.int32, (tiles, 128), 0) * 128 + lax.broadcasted_iota(
        jnp.int32, (tiles, 128), 1
    )
    id_row = lax.shift_right_logical(ids * 4033, 19)
    id_col = ids - id_row * 130
    id_row = jnp.where(slot < counts[0, 0], id_row, -1)
    row_sel = row8 + 1
    col_sel = lax.broadcasted_iota(jnp.int32, (128, 128), 0) + 1
    hot_rows, hot_cols = [], []
    for t in range(tiles):
        hot_rows.append(
            jnp.where(jnp.broadcast_to(id_row[t : t + 1], (8, 128)) == row_sel, 1.0, 0.0).astype(BF16)
        )
        hot_cols.append(
            jnp.where(jnp.broadcast_to(id_col[t : t + 1], (128, 128)) == col_sel, 1.0, 0.0).astype(BF16)
        )
    live = lax.dot_general(
        jnp.concatenate(hot_rows, axis=1),
        jnp.concatenate(hot_cols, axis=1),
        (((1,), (1,)), ((), ())),
        preferred_element_type=F32,
    )
    pltpu.make_async_copy(weights, weights, in_sem.at[1]).wait()
    own[13] = weights[0] * live
    own[14] = weights[1] * live

    pltpu.make_async_copy(own.at[0:13], own.at[0:13], in_sem.at[2]).wait()
    lane_group = jnp.where(
        lane8 < 54, lax.shift_right_logical(lane8 * 57, 9), lax.shift_right_logical(lane8 - 54, 3) + 6
    )
    from_left = jnp.where(lane8 < 54, lane8 - 9 * lane_group, (lane8 - 54) & 7) < 4
    packed = jnp.zeros((8, 128), F32)
    for f in range(FIELDS):
        packed = jnp.where(lane_group == f, pltpu.roll(own[f], base_of(f), 1), packed)
    strip_out[...] = packed

    pl.semaphore_wait(barrier, 4 + len(row_peers) + len(column_peers))

    def remote(src, dst, a, b, i):
        return pltpu.make_async_remote_copy(
            src_ref=src,
            dst_ref=dst,
            send_sem=halo_send.at[i],
            recv_sem=halo_recv.at[i],
            device_id=(a, b),
            device_id_type=MESH,
        )

    halo = [
        remote(strip_out, strips.at[0], px, right, 0),
        remote(strip_out, strips.at[1], px, left, 1),
        remote(own.at[:, 4:8, :], above.at[:, 4:8, :], down, py, 2),
        remote(own.at[:, 0:5, :], below.at[:, 0:5, :], up, py, 3),
        remote(strips.at[0:2], strips.at[2:4], down, py, 4),
        remote(strips.at[0:2], strips.at[4:6], up, py, 5),
    ]
    for copy in halo[:4]:
        copy.start()

    for b in column_peers:
        signal(relay.at[0], px, b)
    rounds = 0
    while 2 << rounds <= n_px // 2:
        rounds += 1

    def pass_on(k):
        if 1 <= k <= rounds:
            pl.semaphore_wait(relay.at[k], 2)
        if k < rounds:
            signal(relay.at[k + 1], at_px(1 << k), py)
            signal(relay.at[k + 1], at_px(-(1 << k)), py)

    pass_on(0)

    loads[6].wait()
    spread = jnp.where(
        lax.shift_right_logical(lax.broadcasted_iota(jnp.int32, (192, 24), 0), 3)
        == lax.broadcasted_iota(jnp.int32, (192, 24), 1),
        1.0,
        0.0,
    ).astype(BF16)
    same_row = (lax.broadcasted_iota(jnp.int32, (192, 192), 0) & 7) == (
        lax.broadcasted_iota(jnp.int32, (192, 192), 1) & 7
    )

    def expand(part):
        tall = jnp.dot(spread, part, preferred_element_type=F32).astype(BF16)
        full = lax.dot_general(tall, spread, (((1,), (1,)), ((), ())), preferred_element_type=F32)
        return jnp.where(same_row, full, 0.0).astype(BF16)

    stiff_all = stiff_v[...]
    stiff_hi = stiff_all.astype(BF16)
    stiff_lo = (stiff_all - stiff_hi.astype(F32)).astype(BF16)
    big_hi, big_lo = expand(stiff_hi), expand(stiff_lo)

    pass_on(1)

    halo[0].wait_recv()
    halo[1].wait_recv()
    for copy in halo[4:]:
        copy.start()
    for copy in halo[2:]:
        copy.wait_recv()

    lower = row8 < 4
    side_mid = jnp.where(from_left, strips[0], strips[1])
    side_above = jnp.where(from_left, strips[2], strips[3])
    side_below = jnp.where(from_left, strips[4], strips[5])
    side_edge = jnp.where(lower, side_below, side_above)
    side_next = pltpu.roll(side_below, 7, 0)

    def unpack(tile, f):
        return pltpu.roll(tile, 128 - base_of(f), 1)

    def extend(first, count):
        fields = range(first, first + count)
        return [
            [own[first : first + count], jnp.stack([unpack(side_mid, f) for f in fields])],
            [
                jnp.where(
                    lax.broadcasted_iota(jnp.int32, (count, 8, 128), 1) < 4,
                    below[first : first + count],
                    above[first : first + count],
                ),
                jnp.stack([unpack(side_edge, f) for f in fields]),
            ],
        ]

    def each(f, *xs):
        return [[f(*[x[t][s] for x in xs]) for s in range(2)] for t in range(2)]

    def shift_rows(x, to, edge):
        r = each(lambda q: pltpu.roll(q, to % 8, 1), x)
        at = lax.broadcasted_iota(jnp.int32, x[0][0].shape, 1) == edge
        return [[jnp.where(at, r[1 - t][s], r[t][s]) for s in range(2)] for t in range(2)]

    def shift_cols(x, to, edge):
        r = each(lambda q: pltpu.roll(q, to % 128, 2), x)
        at = lax.broadcasted_iota(jnp.int32, x[0][0].shape, 2) == edge
        return [[jnp.where(at, r[t][1 - s], r[t][s]) for s in range(2)] for t in range(2)]

    def next_row(x):
        return shift_rows(x, -1, 7)

    def prev_row(x):
        return shift_rows(x, 1, 0)

    def next_col(x):
        return shift_cols(x, -1, 127)

    def prev_col(x):
        return shift_cols(x, 1, 0)

    def add(a, b):
        return each(lambda p, q: p + q, a, b)

    def four_sum(x):
        half = add(x, next_col(x))
        return add(half, next_row(half))

    def to_nodes(x):
        half = add(x, prev_row(x))
        return add(half, prev_col(half))

    u00 = extend(0, 6)
    u01 = next_col(u00)
    u10 = next_row(u00)
    at_three = lax.broadcasted_iota(jnp.int32, (6, 8, 128), 1) == 3
    u10[1] = [
        jnp.where(at_three, pltpu.roll(below[0:6], 7, 1), u10[1][0]),
        jnp.where(at_three, jnp.stack([unpack(side_next, f) for f in range(6)]), u10[1][1]),
    ]
    u11 = next_col(u10)
    corners = (u00, u01, u10, u11)
    field_mass, field_thick, field_added = extend(12, 1), extend(13, 1), extend(14, 1)
    forces = [[[None, None], [None, None]] for _ in range(4)]
    for t in range(2):
        stacked = jnp.concatenate(
            [
                jnp.concatenate([corners[n][t][s][c] for c in range(6) for n in range(4)], axis=0)
                for s in range(2)
            ],
            axis=1,
        )
        hi = stacked.astype(BF16)
        lo = (stacked - hi.astype(F32)).astype(BF16)
        product = (
            jnp.dot(big_hi, lo, preferred_element_type=F32)
            + jnp.dot(big_lo, hi, preferred_element_type=F32)
        ) + jnp.dot(big_hi, hi, preferred_element_type=F32)
        for n in range(4):
            for s in range(2):
                forces[n][t][s] = (
                    jnp.stack(
                        [
                            product[8 * (4 * c + n) : 8 * (4 * c + n) + 8, 128 * s : 128 * s + 128]
                            for c in range(6)
                        ]
                    )
                    * field_thick[t][s]
                )
    pass_on(2)
    internal = add(
        add(forces[0], prev_row(forces[2])), prev_col(add(forces[1], prev_row(forces[3])))
    )

    weight_sum = to_nodes(field_added)
    precond = each(lambda m, w: m + 0.75 * w, field_mass, weight_sum)
    inverse = each(lambda m: 1.0 / m, precond)
    quarter = each(lambda i: 0.25 * i, inverse)
    quarter_weight = each(lambda q, w: q * w, quarter, weight_sum)
    powers = [each(lambda f, g, i: (f - g) * i, extend(6, 6), internal, inverse)]
    for k in range(3):
        p = powers[-1]
        spread_sum = to_nodes(each(lambda a, s: a * s, field_added, four_sum(p)))
        powers.append(
            each(lambda q, n, w, v: q * n - w * v, quarter, spread_sum, quarter_weight, p)
        )

    mine = [x[0][0] for x in powers]
    weighted = [precond[0][0] * x for x in mine]
    moments = [jnp.sum(weighted[k // 2] * mine[k - k // 2], axis=0) for k in range(7)]
    last = four_sum(powers[3])[0][0]
    moments.append(
        0.25
        * jnp.sum(
            field_added[0][0] * (last * last) - weight_sum[0][0] * (mine[3] * mine[3]), axis=0
        )
    )
    sums = jnp.concatenate([jnp.sum(m, axis=0, keepdims=True) for m in moments], axis=0)
    sums = jnp.sum(sums, axis=1, keepdims=True)
    row = jnp.sum(jnp.where(row8 == lane8, sums, 0.0), axis=0, keepdims=True)

    around_mass = four_sum(field_mass)[0][0][0]
    stable = 0.5 * jnp.sqrt((weights[1] + 0.25 * around_mass) / weights[0])
    smallest = jnp.min(jnp.where(live > 0, stable, 1e30), keepdims=True)
    lane1 = lax.broadcasted_iota(jnp.int32, (1, 128), 1)
    row = jnp.where(lane1 == 8, smallest, row)

    if column_peers:
        pl.semaphore_wait(relay.at[0], len(column_peers))

    def gather(row, size, here, src, slots, device, far, i):
        src[...] = row
        slots[pl.ds(here, 1)] = row.reshape(1, 1, 128)
        for k in sorted(range(1, size), key=far):
            pltpu.make_async_remote_copy(
                src_ref=src,
                dst_ref=slots.at[here],
                send_sem=red_send.at[i],
                recv_sem=red_recv.at[i],
                device_id=device(k),
                device_id_type=MESH,
            ).start()
        most = slots.at[pl.ds(0, size - 1)]
        pltpu.make_async_copy(most, most, red_recv.at[i]).wait()
        sums = [slots[k] for k in range(size)]
        lows = sums
        while len(sums) > 1:
            odd = len(sums) % 2
            sums, lows = (
                [sums[j] + sums[j + 1] for j in range(0, len(sums) - odd, 2)] + sums[len(sums) - odd :],
                [jnp.minimum(lows[j], lows[j + 1]) for j in range(0, len(lows) - odd, 2)]
                + lows[len(lows) - odd :],
            )
        return jnp.where(lane1 == 8, lows[0], sums[0])

    def line_far(k):
        return -min(k, n_px - k)

    def plane_far(k):
        x, y = k // 2 % 4, k // 8
        return -(min(x, 4 - x) + min(y, 4 - y))

    row = gather(row, n_py, py, row_plane, got_plane, lambda k: (px, at_py(k)), plane_far, 0)
    for k in range(3, rounds + 1):
        pass_on(k)
    row = gather(row, n_px, px, row_line, got_line, lambda k: (at_px(k), py), line_far, 1)

    row = jnp.broadcast_to(row, (8, 128))
    splat = [jnp.broadcast_to(row[:, k : k + 1], (8, 128)) for k in range(9)]
    accel = coefficients(splat[:8])
    min_step = splat[8]
    total = accel[0] * mine[0]
    for k in range(1, ITERS):
        total = total + accel[k] * mine[k]
    out_gain[...] = min_step * total
    out_step[...] = min_step

    for copy in halo:
        copy.wait_send()
    for i, (slots, size) in enumerate(((got_plane, n_py), (got_line, n_px))):
        most = slots.at[pl.ds(0, size - 1)]
        pltpu.make_async_copy(most, most, red_send.at[i]).wait()


def local(n_px, n_py, disp, vel, force, mass, thick, added, stiff, elements, counts):
    tiles = elements.shape[0]
    vmem = lambda *dims: pltpu.VMEM(dims, F32)
    dma = lambda n: pltpu.SemaphoreType.DMA((n,))
    gain, step = pl.pallas_call(
        functools.partial(kernel, n_px, n_py),
        out_shape=[jax.ShapeDtypeStruct(disp.shape, F32), jax.ShapeDtypeStruct((8, 128), F32)],
        in_specs=[pl.BlockSpec(memory_space=pltpu.HBM)] * 7 + [pl.BlockSpec(memory_space=pltpu.SMEM)],
        out_specs=[pl.BlockSpec(memory_space=pltpu.VMEM)] * 2,
        scratch_shapes=[
            vmem(FIELDS, 8, 128),
            vmem(2, 8, 128),
            vmem(24, 24),
            pltpu.VMEM((tiles, 128), jnp.int32),
            vmem(FIELDS, 8, 128),
            vmem(FIELDS, 8, 128),
            vmem(8, 128),
            vmem(6, 8, 128),
            vmem(1, 128),
            vmem(1, 128),
            vmem(n_py, 1, 128),
            vmem(n_px, 1, 128),
            dma(4),
            dma(6),
            dma(6),
            dma(2),
            dma(2),
            pltpu.SemaphoreType.REGULAR((4,)),
        ],
        compiler_params=pltpu.CompilerParams(
            collective_id=0, has_side_effects=True, vmem_limit_bytes=8 << 20
        ),
        name="crash_step",
    )(*(pltpu.with_memory_space_constraint(x, pltpu.HBM) for x in (disp, force, mass, thick, added, stiff, elements)), counts)
    new_velocity = vel + gain
    new_displacement = disp + step * new_velocity
    return new_velocity, new_displacement


def solution(mesh):
    field = P(None, "px", "py")
    plane = P("px", "py")
    return jax.shard_map(
        functools.partial(local, mesh.shape["px"], mesh.shape["py"]),
        mesh=mesh,
        in_specs=(field, field, field, plane, plane, plane, P(), plane, plane),
        out_specs=(field, field),
        check_vma=False,
    )
```

```python
import functools

import jax
import jax.numpy as jnp
from jax import lax
from jax.experimental import pallas as pl
from jax.experimental.pallas import tpu as pltpu
from jax.sharding import PartitionSpec as P

ITERS = 4
FIELDS = 15
MESH = pl.DeviceIdType.MESH
F32 = jnp.float32
BF16 = jnp.bfloat16


def quadratic(left, right, moments):
    total = None
    for i, a in enumerate(left):
        inner = None
        for j, b in enumerate(right):
            term = b * moments[i + j]
            inner = term if inner is None else inner + term
        total = a * inner if total is None else total + a * inner
    return total


def coefficients(mu):
    one = jnp.ones_like(mu[0])
    zero = jnp.zeros_like(mu[0])
    energy = [mu[k] - mu[k + 1] for k in range(7)]
    scaled, direction = [one], [one]
    gamma = mu[0]
    accel = [zero] * ITERS
    for sweep in range(ITERS):
        curvature = quadratic(direction, direction, energy)
        step = jnp.clip(gamma / curvature, 0.74, 26.0)
        for i, d in enumerate(direction):
            accel[i] = accel[i] + step * d
        if sweep + 1 < ITERS:
            applied = direction + [zero]
            for i, d in enumerate(direction):
                applied[i + 1] = applied[i + 1] - d
            scaled = [s - step * a for s, a in zip(scaled + [zero], applied)]
            gamma_next = jnp.maximum(quadratic(scaled, scaled, mu), 0.0)
            ratio = gamma_next / gamma
            direction = [s + ratio * d for s, d in zip(scaled, direction + [zero])]
            gamma = gamma_next
    return accel


def width_of(f):
    return 9 if f < 6 or f > 12 else 8


ORDER = [0, 1, 2, 3, 4, 5, 13, 14, 6, 7, 8, 9, 10, 11, 12]
BASE = {f: sum(width_of(g) for g in ORDER[: ORDER.index(f)]) for f in ORDER}


def kernel(
    n_px,
    n_py,
    disp,
    force,
    mass,
    thick,
    added,
    stiff,
    elements,
    counts,
    out_gain,
    out_step,
    own,
    weights,
    stiff_v,
    elem_v,
    above,
    below,
    strip_out,
    strips_left,
    strips_right,
    row_plane,
    row_line,
    got_plane,
    got_line,
    in_sem,
    halo_send,
    halo_recv,
    red_send,
    red_recv,
    relay,
):
    px = lax.axis_index("px")
    py = lax.axis_index("py")

    def at_px(k):
        return lax.rem(px + (n_px + k), n_px)

    def at_py(k):
        return lax.rem(py + (n_py + k), n_py)

    loads = [
        pltpu.make_async_copy(src, dst, in_sem.at[i])
        for src, dst, i in (
            (elements, elem_v, 0),
            (thick, weights.at[0], 1),
            (added, weights.at[1], 1),
            (disp, own.at[0:6], 2),
            (force, own.at[6:12], 2),
            (mass, own.at[12], 2),
            (stiff, stiff_v, 3),
        )
    ]
    for load in loads:
        load.start()

    up, down, left, right = at_px(-1), at_px(1), at_py(-1), at_py(1)
    barrier = pltpu.get_barrier_semaphore()

    def signal(sem, a, b):
        pl.semaphore_signal(sem, inc=1, device_id=(a, b), device_id_type=MESH)

    span = n_py // 4 if n_py >= 8 else n_py
    n_x, n_y = span // 2, n_py // span
    core, chip_x, chip_y = lax.rem(py, 2), lax.div(lax.rem(py, span), 2), lax.div(py, span)

    def in_plane(dx, dy, other=False):
        x = lax.rem(chip_x + (n_x + dx), n_x)
        y = lax.rem(chip_y + (n_y + dy), n_y)
        return y * span + x * 2 + (1 - core if other else core)

    row_peers = [in_plane(1, 0), in_plane(-1, 0)]
    column_peers = [in_plane(0, 1), in_plane(0, -1)] if n_y > 1 else []
    beside = row_peers + [in_plane(1, 0, True), in_plane(-1, 0, True)] + column_peers
    signal(barrier, px, right)
    signal(barrier, px, left)
    for a in (up, down):
        signal(barrier, a, py)
    for b in beside:
        signal(barrier, px, b)

    row8 = lax.broadcasted_iota(jnp.int32, (8, 128), 0)
    lane8 = lax.broadcasted_iota(jnp.int32, (8, 128), 1)

    loads[0].wait()
    ids = elem_v[...]
    tiles = ids.shape[0]
    slot = lax.broadcasted_iota(jnp.int32, (tiles, 128), 0) * 128 + lax.broadcasted_iota(
        jnp.int32, (tiles, 128), 1
    )
    id_row = lax.shift_right_logical(ids * 4033, 19)
    id_col = ids - id_row * 130
    id_row = jnp.where(slot < counts[0, 0], id_row, -1)
    row_sel = row8 + 1
    col_sel = lax.broadcasted_iota(jnp.int32, (128, 128), 0) + 1
    hot_rows, hot_cols = [], []
    for t in range(tiles):
        hot_rows.append(
            jnp.where(jnp.broadcast_to(id_row[t : t + 1], (8, 128)) == row_sel, 1.0, 0.0).astype(BF16)
        )
        hot_cols.append(
            jnp.where(jnp.broadcast_to(id_col[t : t + 1], (128, 128)) == col_sel, 1.0, 0.0).astype(BF16)
        )
    live = lax.dot_general(
        jnp.concatenate(hot_rows, axis=1),
        jnp.concatenate(hot_cols, axis=1),
        (((1,), (1,)), ((), ())),
        preferred_element_type=F32,
    )
    pltpu.make_async_copy(weights, weights, in_sem.at[1]).wait()
    own[13] = weights[0] * live
    own[14] = weights[1] * live

    pltpu.make_async_copy(own.at[0:13], own.at[0:13], in_sem.at[2]).wait()
    to_right = jnp.zeros((8, 128), F32)
    to_left = jnp.zeros((8, 128), F32)
    for f in range(FIELDS):
        field = own[f]
        start, end = BASE[f], BASE[f] + width_of(f)
        to_right = jnp.where(
            (lane8 >= start) & (lane8 < end), pltpu.roll(field, end % 128, 1), to_right
        )
        to_left = jnp.where(
            (lane8 >= 5 * f) & (lane8 < 5 * f + 5), pltpu.roll(field, 5 * f, 1), to_left
        )
    strip_out[0] = to_right
    strip_out[1] = to_left

    pl.semaphore_wait(barrier, 4 + len(beside))

    def remote(src, dst, a, b, i):
        return pltpu.make_async_remote_copy(
            src_ref=src,
            dst_ref=dst,
            send_sem=halo_send.at[i],
            recv_sem=halo_recv.at[i],
            device_id=(a, b),
            device_id_type=MESH,
        )

    halo = [
        remote(strip_out.at[0], strips_left.at[0], px, right, 0),
        remote(own.at[:, 4:8, :], above.at[:, 4:8, :], down, py, 1),
        remote(own.at[:, 0:5, :], below.at[:, 0:5, :], up, py, 2),
        remote(strip_out.at[1], strips_right.at[0], px, left, 3),
        remote(strips_left.at[0], strips_left.at[1], down, py, 4),
        remote(strips_left.at[0], strips_left.at[2], up, py, 5),
        remote(strips_right.at[0], strips_right.at[1], down, py, 6),
        remote(strips_right.at[0], strips_right.at[2], up, py, 7),
    ]
    for copy in halo[:4]:
        copy.start()

    def plane_round(k):
        if k >= 1 and (k == 1 or column_peers):
            pl.semaphore_wait(relay.at[k - 1], 2)
        if k == 0:
            for b in row_peers:
                signal(relay.at[0], px, b)
        elif k < 3:
            for b in column_peers:
                signal(relay.at[k], px, b)

    plane_round(0)
    rounds = 0
    while 2 << rounds <= n_px // 2:
        rounds += 1

    def pass_on(k):
        if 1 <= k <= rounds:
            pl.semaphore_wait(relay.at[2 + k], 2)
        if k < rounds:
            signal(relay.at[3 + k], at_px(1 << k), py)
            signal(relay.at[3 + k], at_px(-(1 << k)), py)

    pass_on(0)

    loads[6].wait()
    spread = jnp.where(
        lax.shift_right_logical(lax.broadcasted_iota(jnp.int32, (192, 24), 0), 3)
        == lax.broadcasted_iota(jnp.int32, (192, 24), 1),
        1.0,
        0.0,
    ).astype(BF16)
    same_row = (lax.broadcasted_iota(jnp.int32, (192, 192), 0) & 7) == (
        lax.broadcasted_iota(jnp.int32, (192, 192), 1) & 7
    )

    def expand(part):
        tall = jnp.dot(spread, part, preferred_element_type=F32).astype(BF16)
        full = lax.dot_general(tall, spread, (((1,), (1,)), ((), ())), preferred_element_type=F32)
        return jnp.where(same_row, full, 0.0).astype(BF16)

    stiff_all = stiff_v[...]
    stiff_hi = stiff_all.astype(BF16)
    stiff_lo = (stiff_all - stiff_hi.astype(F32)).astype(BF16)
    big_hi, big_lo = expand(stiff_hi), expand(stiff_lo)

    pass_on(1)
    plane_round(1)

    halo[0].wait_recv()
    halo[4].start()
    halo[5].start()
    plane_round(2)
    for i in (1, 2, 4, 5):
        halo[i].wait_recv()

    lower = row8 < 4

    def edges(strips):
        return strips[0], jnp.where(lower, strips[2], strips[1]), pltpu.roll(strips[2], 7, 0)

    lefts = edges(strips_left)
    rights = None

    def side(i, f):
        column = pltpu.roll(lefts[i], (128 - BASE[f] - width_of(f)) % 128, 1)
        if rights is not None:
            column = jnp.where(lane8 < 5, pltpu.roll(rights[i], (128 - 5 * f) % 128, 1), column)
        return column

    def extend(first, count):
        fields = range(first, first + count)
        return [
            [own[first : first + count], jnp.stack([side(0, f) for f in fields])],
            [
                jnp.where(
                    lax.broadcasted_iota(jnp.int32, (count, 8, 128), 1) < 4,
                    below[first : first + count],
                    above[first : first + count],
                ),
                jnp.stack([side(1, f) for f in fields]),
            ],
        ]

    def each(f, *xs):
        return [[f(*[x[t][s] for x in xs]) for s in range(2)] for t in range(2)]

    def shift_rows(x, to, edge):
        r = each(lambda q: pltpu.roll(q, to % 8, 1), x)
        at = lax.broadcasted_iota(jnp.int32, x[0][0].shape, 1) == edge
        return [[jnp.where(at, r[1 - t][s], r[t][s]) for s in range(2)] for t in range(2)]

    def shift_cols(x, to, edge):
        r = each(lambda q: pltpu.roll(q, to % 128, 2), x)
        at = lax.broadcasted_iota(jnp.int32, x[0][0].shape, 2) == edge
        return [[jnp.where(at, r[t][1 - s], r[t][s]) for s in range(2)] for t in range(2)]

    def next_row(x):
        return shift_rows(x, -1, 7)

    def prev_row(x):
        return shift_rows(x, 1, 0)

    def next_col(x):
        return shift_cols(x, -1, 127)

    def prev_col(x):
        return shift_cols(x, 1, 0)

    def add(a, b):
        return each(lambda p, q: p + q, a, b)

    def four_sum(x):
        half = add(x, next_col(x))
        return add(half, next_row(half))

    def to_nodes(x):
        half = add(x, prev_row(x))
        return add(half, prev_col(half))

    def solve():
        u00 = extend(0, 6)
        u01 = next_col(u00)
        u10 = next_row(u00)
        at_three = lax.broadcasted_iota(jnp.int32, (6, 8, 128), 1) == 3
        u10[1] = [
            jnp.where(at_three, pltpu.roll(below[0:6], 7, 1), u10[1][0]),
            jnp.where(at_three, jnp.stack([side(2, f) for f in range(6)]), u10[1][1]),
        ]
        u11 = next_col(u10)
        corners = (u00, u01, u10, u11)
        field_mass, field_thick, field_added = extend(12, 1), extend(13, 1), extend(14, 1)
        forces = [[[None, None], [None, None]] for _ in range(4)]
        for t in range(2):
            stacked = jnp.concatenate(
                [
                    jnp.concatenate([corners[n][t][s][c] for c in range(6) for n in range(4)], axis=0)
                    for s in range(2)
                ],
                axis=1,
            )
            hi = stacked.astype(BF16)
            lo = (stacked - hi.astype(F32)).astype(BF16)
            product = (
                jnp.dot(big_hi, lo, preferred_element_type=F32)
                + jnp.dot(big_lo, hi, preferred_element_type=F32)
            ) + jnp.dot(big_hi, hi, preferred_element_type=F32)
            for n in range(4):
                for s in range(2):
                    forces[n][t][s] = (
                        jnp.stack(
                            [
                                product[8 * (4 * c + n) : 8 * (4 * c + n) + 8, 128 * s : 128 * s + 128]
                                for c in range(6)
                            ]
                        )
                        * field_thick[t][s]
                    )
        internal = add(
            add(forces[0], prev_row(forces[2])), prev_col(add(forces[1], prev_row(forces[3])))
        )

        weight_sum = to_nodes(field_added)
        precond = each(lambda m, w: m + 0.75 * w, field_mass, weight_sum)
        inverse = each(lambda m: 1.0 / m, precond)
        quarter = each(lambda i: 0.25 * i, inverse)
        quarter_weight = each(lambda q, w: q * w, quarter, weight_sum)
        powers = [each(lambda f, g, i: (f - g) * i, extend(6, 6), internal, inverse)]
        for k in range(3):
            p = powers[-1]
            spread_sum = to_nodes(each(lambda a, s: a * s, field_added, four_sum(p)))
            powers.append(
                each(lambda q, n, w, v: q * n - w * v, quarter, spread_sum, quarter_weight, p)
            )
        return powers, precond, weight_sum, field_mass, field_thick, field_added

    powers, precond, weight_sum, field_mass, field_thick, field_added = solve()
    pass_on(2)

    def range_of(x):
        return jnp.where(lax.broadcasted_iota(jnp.int32, x[0][0].shape, 2) < 123, x[0][0], x[0][1])

    part = [range_of(x) for x in powers]
    mass_part, sum_part, added_part = range_of(precond), range_of(weight_sum), range_of(field_added)
    weighted = [mass_part * x for x in part]
    moments = [jnp.sum(weighted[k // 2] * part[k - k // 2], axis=0) for k in range(7)]
    last = range_of(four_sum(powers[3]))
    moments.append(
        0.25 * jnp.sum(added_part * (last * last) - sum_part * (part[3] * part[3]), axis=0)
    )
    sums = jnp.concatenate([jnp.sum(m, axis=0, keepdims=True) for m in moments], axis=0)
    sums = jnp.sum(sums, axis=1, keepdims=True)
    row = jnp.sum(jnp.where(row8 == lane8, sums, 0.0), axis=0, keepdims=True)

    added_part = added_part[0]
    stable = 0.5 * jnp.sqrt(
        (added_part + 0.25 * range_of(four_sum(field_mass))[0]) / range_of(field_thick)[0]
    )
    smallest = jnp.min(jnp.where(added_part > 0, stable, 1e30), keepdims=True)
    lane1 = lax.broadcasted_iota(jnp.int32, (1, 128), 1)
    row = jnp.where(lane1 == 8, smallest, row)

    plane_round(3)

    def spread_row(row, size, here, src, slots, device, far, i):
        src[...] = row
        slots[pl.ds(here, 1)] = row.reshape(1, 1, 128)
        for k in sorted(range(1, size), key=far):
            pltpu.make_async_remote_copy(
                src_ref=src,
                dst_ref=slots.at[here],
                send_sem=red_send.at[i],
                recv_sem=red_recv.at[i],
                device_id=device(k),
                device_id_type=MESH,
            ).start()

    def collect(size, slots, i):
        most = slots.at[pl.ds(0, size - 1)]
        pltpu.make_async_copy(most, most, red_recv.at[i]).wait()
        sums = [slots[k] for k in range(size)]
        lows = sums
        while len(sums) > 1:
            odd = len(sums) % 2
            sums, lows = (
                [sums[j] + sums[j + 1] for j in range(0, len(sums) - odd, 2)] + sums[len(sums) - odd :],
                [jnp.minimum(lows[j], lows[j + 1]) for j in range(0, len(lows) - odd, 2)]
                + lows[len(lows) - odd :],
            )
        return jnp.where(lane1 == 8, lows[0], sums[0])

    def line_far(k):
        return -min(k, n_px - k)

    def plane_far(k):
        x, y = k // 2 % 4, k // 8
        return -(min(x, 4 - x) + min(y, 4 - y))

    spread_row(row, n_py, py, row_plane, got_plane, lambda k: (px, at_py(k)), plane_far, 0)
    halo[3].wait_recv()
    halo[6].start()
    halo[7].start()
    row = collect(n_py, got_plane, 0)
    for k in range(3, rounds + 1):
        pass_on(k)
    spread_row(row, n_px, px, row_line, got_line, lambda k: (at_px(k), py), line_far, 1)

    halo[6].wait_recv()
    halo[7].wait_recv()
    rights = edges(strips_right)
    mine = [x[0][0] for x in solve()[0]]
    row = collect(n_px, got_line, 1)

    row = jnp.broadcast_to(row, (8, 128))
    splat = [jnp.broadcast_to(row[:, k : k + 1], (8, 128)) for k in range(9)]
    accel = coefficients(splat[:8])
    min_step = splat[8]
    total = accel[0] * mine[0]
    for k in range(1, ITERS):
        total = total + accel[k] * mine[k]
    out_gain[...] = min_step * total
    out_step[...] = min_step

    for copy in halo:
        copy.wait_send()
    for i, (slots, size) in enumerate(((got_plane, n_py), (got_line, n_px))):
        most = slots.at[pl.ds(0, size - 1)]
        pltpu.make_async_copy(most, most, red_send.at[i]).wait()


def local(n_px, n_py, disp, vel, force, mass, thick, added, stiff, elements, counts):
    tiles = elements.shape[0]
    vmem = lambda *dims: pltpu.VMEM(dims, F32)
    dma = lambda n: pltpu.SemaphoreType.DMA((n,))
    gain, step = pl.pallas_call(
        functools.partial(kernel, n_px, n_py),
        out_shape=[jax.ShapeDtypeStruct(disp.shape, F32), jax.ShapeDtypeStruct((8, 128), F32)],
        in_specs=[pl.BlockSpec(memory_space=pltpu.HBM)] * 7 + [pl.BlockSpec(memory_space=pltpu.SMEM)],
        out_specs=[pl.BlockSpec(memory_space=pltpu.VMEM)] * 2,
        scratch_shapes=[
            vmem(FIELDS, 8, 128),
            vmem(2, 8, 128),
            vmem(24, 24),
            pltpu.VMEM((tiles, 128), jnp.int32),
            vmem(FIELDS, 8, 128),
            vmem(FIELDS, 8, 128),
            vmem(2, 8, 128),
            vmem(3, 8, 128),
            vmem(3, 8, 128),
            vmem(1, 128),
            vmem(1, 128),
            vmem(n_py, 1, 128),
            vmem(n_px, 1, 128),
            dma(4),
            dma(8),
            dma(8),
            dma(2),
            dma(2),
            pltpu.SemaphoreType.REGULAR((6,)),
        ],
        compiler_params=pltpu.CompilerParams(
            collective_id=0, has_side_effects=True, vmem_limit_bytes=8 << 20
        ),
        name="crash_step",
    )(*(pltpu.with_memory_space_constraint(x, pltpu.HBM) for x in (disp, force, mass, thick, added, stiff, elements)), counts)
    new_velocity = vel + gain
    new_displacement = disp + step * new_velocity
    return new_velocity, new_displacement


def solution(mesh):
    field = P(None, "px", "py")
    plane = P("px", "py")
    return jax.shard_map(
        functools.partial(local, mesh.shape["px"], mesh.shape["py"]),
        mesh=mesh,
        in_specs=(field, field, field, plane, plane, plane, P(), plane, plane),
        out_specs=(field, field),
        check_vma=False,
    )
```

```python
import functools

import jax
import jax.numpy as jnp
from jax import lax
from jax.experimental import pallas as pl
from jax.experimental.pallas import tpu as pltpu
from jax.sharding import PartitionSpec as P

ITERS = 4
FIELDS = 15
MESH = pl.DeviceIdType.MESH
F32 = jnp.float32
BF16 = jnp.bfloat16


def quadratic(left, right, moments):
    total = None
    for i, a in enumerate(left):
        inner = None
        for j, b in enumerate(right):
            term = b * moments[i + j]
            inner = term if inner is None else inner + term
        total = a * inner if total is None else total + a * inner
    return total


def coefficients(mu):
    one = jnp.ones_like(mu[0])
    zero = jnp.zeros_like(mu[0])
    energy = [mu[k] - mu[k + 1] for k in range(7)]
    scaled, direction = [one], [one]
    gamma = mu[0]
    accel = [zero] * ITERS
    for sweep in range(ITERS):
        curvature = quadratic(direction, direction, energy)
        step = jnp.clip(gamma / curvature, 0.74, 26.0)
        for i, d in enumerate(direction):
            accel[i] = accel[i] + step * d
        if sweep + 1 < ITERS:
            applied = direction + [zero]
            for i, d in enumerate(direction):
                applied[i + 1] = applied[i + 1] - d
            scaled = [s - step * a for s, a in zip(scaled + [zero], applied)]
            gamma_next = jnp.maximum(quadratic(scaled, scaled, mu), 0.0)
            ratio = gamma_next / gamma
            direction = [s + ratio * d for s, d in zip(scaled, direction + [zero])]
            gamma = gamma_next
    return accel


def width_of(f):
    return 9 if f < 6 or f > 12 else 8


ORDER = [0, 1, 2, 3, 4, 5, 13, 14, 6, 7, 8, 9, 10, 11, 12]
BASE = {f: sum(width_of(g) for g in ORDER[: ORDER.index(f)]) for f in ORDER}


def kernel(
    n_px,
    n_py,
    disp,
    force,
    mass,
    thick,
    added,
    stiff,
    elements,
    counts,
    out_gain,
    out_step,
    own,
    weights,
    stiff_v,
    elem_v,
    above,
    below,
    strip_out,
    strips_left,
    strips_right,
    row_plane,
    row_line,
    got_plane,
    got_line,
    in_sem,
    halo_send,
    halo_recv,
    red_send,
    red_recv,
    relay,
):
    px = lax.axis_index("px")
    py = lax.axis_index("py")

    def at_px(k):
        return lax.rem(px + (n_px + k), n_px)

    def at_py(k):
        return lax.rem(py + (n_py + k), n_py)

    loads = [
        pltpu.make_async_copy(src, dst, in_sem.at[i])
        for src, dst, i in (
            (elements, elem_v, 0),
            (thick, weights.at[0], 1),
            (added, weights.at[1], 1),
            (disp, own.at[0:6], 2),
            (force, own.at[6:12], 2),
            (mass, own.at[12], 2),
            (stiff, stiff_v, 3),
        )
    ]
    for load in loads:
        load.start()

    up, down, left, right = at_px(-1), at_px(1), at_py(-1), at_py(1)
    barrier = pltpu.get_barrier_semaphore()

    def signal(sem, a, b):
        pl.semaphore_signal(sem, inc=1, device_id=(a, b), device_id_type=MESH)

    span = n_py // 4 if n_py >= 8 else n_py
    n_x, n_y = span // 2, n_py // span
    core, chip_x, chip_y = lax.rem(py, 2), lax.div(lax.rem(py, span), 2), lax.div(py, span)

    def in_plane(dx, dy, other=False):
        x = lax.rem(chip_x + (n_x + dx), n_x)
        y = lax.rem(chip_y + (n_y + dy), n_y)
        return y * span + x * 2 + (1 - core if other else core)

    row_peers = [in_plane(1, 0), in_plane(-1, 0)]
    column_peers = [in_plane(0, 1), in_plane(0, -1)] if n_y > 1 else []
    beside = row_peers + [in_plane(1, 0, True), in_plane(-1, 0, True)] + column_peers
    signal(barrier, px, right)
    signal(barrier, px, left)
    for a in (up, down):
        signal(barrier, a, py)
    for b in beside:
        signal(barrier, px, b)

    row8 = lax.broadcasted_iota(jnp.int32, (8, 128), 0)
    lane8 = lax.broadcasted_iota(jnp.int32, (8, 128), 1)

    loads[0].wait()
    ids = elem_v[...]
    tiles = ids.shape[0]
    slot = lax.broadcasted_iota(jnp.int32, (tiles, 128), 0) * 128 + lax.broadcasted_iota(
        jnp.int32, (tiles, 128), 1
    )
    id_row = lax.shift_right_logical(ids * 4033, 19)
    id_col = ids - id_row * 130
    id_row = jnp.where(slot < counts[0, 0], id_row, -1)
    row_sel = row8 + 1
    col_sel = lax.broadcasted_iota(jnp.int32, (128, 128), 0) + 1
    hot_rows, hot_cols = [], []
    for t in range(tiles):
        hot_rows.append(
            jnp.where(jnp.broadcast_to(id_row[t : t + 1], (8, 128)) == row_sel, 1.0, 0.0).astype(BF16)
        )
        hot_cols.append(
            jnp.where(jnp.broadcast_to(id_col[t : t + 1], (128, 128)) == col_sel, 1.0, 0.0).astype(BF16)
        )
    live = lax.dot_general(
        jnp.concatenate(hot_rows, axis=1),
        jnp.concatenate(hot_cols, axis=1),
        (((1,), (1,)), ((), ())),
        preferred_element_type=F32,
    )
    pltpu.make_async_copy(weights, weights, in_sem.at[1]).wait()
    own[13] = weights[0] * live
    own[14] = weights[1] * live

    pltpu.make_async_copy(own.at[0:13], own.at[0:13], in_sem.at[2]).wait()
    to_right = jnp.zeros((8, 128), F32)
    to_left = jnp.zeros((8, 128), F32)
    for f in range(FIELDS):
        field = own[f]
        start, end = BASE[f], BASE[f] + width_of(f)
        to_right = jnp.where(
            (lane8 >= start) & (lane8 < end), pltpu.roll(field, end % 128, 1), to_right
        )
        to_left = jnp.where(
            (lane8 >= 5 * f) & (lane8 < 5 * f + 5), pltpu.roll(field, 5 * f, 1), to_left
        )
    strip_out[0] = to_right
    strip_out[1] = to_left

    pl.semaphore_wait(barrier, 4 + len(beside))

    def remote(src, dst, a, b, i):
        return pltpu.make_async_remote_copy(
            src_ref=src,
            dst_ref=dst,
            send_sem=halo_send.at[i],
            recv_sem=halo_recv.at[i],
            device_id=(a, b),
            device_id_type=MESH,
        )

    halo = [
        remote(strip_out.at[0], strips_left.at[0], px, right, 0),
        remote(own.at[:, 4:8, :], above.at[:, 4:8, :], down, py, 1),
        remote(own.at[:, 0:5, :], below.at[:, 0:5, :], up, py, 2),
        remote(strip_out.at[1], strips_right.at[0], px, left, 3),
        remote(strips_left.at[0], strips_left.at[1], down, py, 4),
        remote(strips_left.at[0], strips_left.at[2], up, py, 5),
        remote(strips_right.at[0], strips_right.at[1], down, py, 6),
        remote(strips_right.at[0], strips_right.at[2], up, py, 7),
    ]
    for copy in halo[:4]:
        copy.start()

    def plane_round(k):
        if k >= 1 and (k == 1 or column_peers):
            pl.semaphore_wait(relay.at[k - 1], 2)
        if k == 0:
            for b in row_peers:
                signal(relay.at[0], px, b)
        elif k < 3:
            for b in column_peers:
                signal(relay.at[k], px, b)

    plane_round(0)
    rounds = 0
    while 2 << rounds <= n_px // 2:
        rounds += 1

    def pass_on(k):
        if 1 <= k <= rounds:
            pl.semaphore_wait(relay.at[2 + k], 2)
        if k < rounds:
            signal(relay.at[3 + k], at_px(1 << k), py)
            signal(relay.at[3 + k], at_px(-(1 << k)), py)

    pass_on(0)

    loads[6].wait()
    spread = jnp.where(
        lax.shift_right_logical(lax.broadcasted_iota(jnp.int32, (192, 24), 0), 3)
        == lax.broadcasted_iota(jnp.int32, (192, 24), 1),
        1.0,
        0.0,
    ).astype(BF16)
    same_row = (lax.broadcasted_iota(jnp.int32, (192, 192), 0) & 7) == (
        lax.broadcasted_iota(jnp.int32, (192, 192), 1) & 7
    )

    def expand(part):
        tall = jnp.dot(spread, part, preferred_element_type=F32).astype(BF16)
        full = lax.dot_general(tall, spread, (((1,), (1,)), ((), ())), preferred_element_type=F32)
        return jnp.where(same_row, full, 0.0).astype(BF16)

    stiff_all = stiff_v[...]
    stiff_hi = stiff_all.astype(BF16)
    stiff_lo = (stiff_all - stiff_hi.astype(F32)).astype(BF16)
    big_hi, big_lo = expand(stiff_hi), expand(stiff_lo)

    pass_on(1)
    plane_round(1)

    halo[0].wait_recv()
    halo[4].start()
    halo[5].start()
    plane_round(2)
    halo[1].wait_recv()
    halo[2].wait_recv()
    lower = row8 < 4

    def extend(beside, first, count):
        edge = jnp.where(
            lax.broadcasted_iota(jnp.int32, (count, 8, 128), 1) < 4,
            below[first : first + count],
            above[first : first + count],
        )
        tiles = [own[first : first + count], edge]
        if beside is None:
            return tiles
        return [
            jnp.stack([beside(i, first + c, x[c]) for c in range(count)]) for i, x in enumerate(tiles)
        ]

    def each(f, *xs):
        return [f(*[x[t] for x in xs]) for t in range(2)]

    def shift_rows(x, to, edge):
        r = each(lambda q: pltpu.roll(q, to % 8, 1), x)
        at = lax.broadcasted_iota(jnp.int32, x[0].shape, 1) == edge
        return [jnp.where(at, r[1 - t], r[t]) for t in range(2)]

    def next_row(x):
        return shift_rows(x, -1, 7)

    def prev_row(x):
        return shift_rows(x, 1, 0)

    def next_col(x):
        return each(lambda q: pltpu.roll(q, 127, 2), x)

    def prev_col(x):
        return each(lambda q: pltpu.roll(q, 1, 2), x)

    def add(a, b):
        return each(lambda p, q: p + q, a, b)

    def four_sum(x):
        half = add(x, next_col(x))
        return add(half, next_row(half))

    def to_nodes(x):
        half = add(x, prev_row(x))
        return add(half, prev_col(half))

    def solve(beside):
        u00 = extend(beside, 0, 6)
        u01 = next_col(u00)
        u10 = next_row(u00)
        row_12 = pltpu.roll(below[0:6], 7, 1)
        if beside is not None:
            row_12 = jnp.stack([beside(2, c, row_12[c]) for c in range(6)])
        at_three = lax.broadcasted_iota(jnp.int32, (6, 8, 128), 1) == 3
        u10[1] = jnp.where(at_three, row_12, u10[1])
        u11 = next_col(u10)
        corners = (u00, u01, u10, u11)
        field_mass, field_thick, field_added = (extend(beside, f, 1) for f in (12, 13, 14))
        stacked = jnp.concatenate(
            [
                jnp.concatenate([corners[n][t][c] for c in range(6) for n in range(4)], axis=0)
                for t in range(2)
            ],
            axis=1,
        )
        hi = stacked.astype(BF16)
        lo = (stacked - hi.astype(F32)).astype(BF16)
        product = (
            jnp.dot(big_hi, lo, preferred_element_type=F32)
            + jnp.dot(big_lo, hi, preferred_element_type=F32)
        ) + jnp.dot(big_hi, hi, preferred_element_type=F32)
        forces = [
            [
                jnp.stack(
                    [
                        product[8 * (4 * c + n) : 8 * (4 * c + n) + 8, 128 * t : 128 * t + 128]
                        for c in range(6)
                    ]
                )
                * field_thick[t]
                for t in range(2)
            ]
            for n in range(4)
        ]
        internal = add(
            add(forces[0], prev_row(forces[2])), prev_col(add(forces[1], prev_row(forces[3])))
        )
        weight_sum = to_nodes(field_added)
        precond = each(lambda m, w: m + 0.75 * w, field_mass, weight_sum)
        inverse = each(lambda m: 1.0 / m, precond)
        quarter = each(lambda i: 0.25 * i, inverse)
        quarter_weight = each(lambda q, w: q * w, quarter, weight_sum)
        powers = [
            each(lambda f, g, i: (f - g) * i, extend(beside, 6, 6), internal, inverse)
        ]
        for k in range(3):
            p = powers[-1]
            spread_sum = to_nodes(each(lambda a, s: a * s, field_added, four_sum(p)))
            powers.append(
                each(lambda q, n, w, v: q * n - w * v, quarter, spread_sum, quarter_weight, p)
            )
        out = powers + [four_sum(powers[3]), precond, weight_sum, field_added, field_thick]
        return [x[0] for x in out] + [four_sum(field_mass)[0]]

    inner = solve(None)

    pass_on(2)
    plane_round(3)
    halo[4].wait_recv()
    halo[5].wait_recv()

    def edges(strips):
        return strips[0], jnp.where(lower, strips[2], strips[1]), pltpu.roll(strips[2], 7, 0)

    def columns_left(tiles):
        return lambda i, f, x: jnp.where(
            lane8 >= 119, pltpu.roll(tiles[i], (128 - BASE[f] - width_of(f)) % 128, 1), x
        )

    def columns_right(tiles):
        return lambda i, f, x: jnp.where(
            lane8 < 5, pltpu.roll(tiles[i], (128 - 5 * f) % 128, 1), x
        )

    outer = solve(columns_left(edges(strips_left)))

    def merge(a, b):
        lane = lax.broadcasted_iota(jnp.int32, a.shape, 2)
        return jnp.where((lane >= 4) & (lane < 123), a, b)

    merged = [merge(a, b) for a, b in zip(inner, outer)]
    part, last = merged[:4], merged[4]
    mass_part, sum_part, added_part, thick_part, around_part = merged[5:]
    weighted = [mass_part * x for x in part]
    moments = [jnp.sum(weighted[k // 2] * part[k - k // 2], axis=0) for k in range(7)]
    moments.append(
        0.25 * jnp.sum(added_part * (last * last) - sum_part * (part[3] * part[3]), axis=0)
    )
    sums = jnp.concatenate([jnp.sum(m, axis=0, keepdims=True) for m in moments], axis=0)
    sums = jnp.sum(sums, axis=1, keepdims=True)
    row = jnp.sum(jnp.where(row8 == lane8, sums, 0.0), axis=0, keepdims=True)

    added_part = added_part[0]
    stable = 0.5 * jnp.sqrt((added_part + 0.25 * around_part[0]) / thick_part[0])
    smallest = jnp.min(jnp.where(added_part > 0, stable, 1e30), keepdims=True)
    lane1 = lax.broadcasted_iota(jnp.int32, (1, 128), 1)
    row = jnp.where(lane1 == 8, smallest, row)

    def spread_row(row, size, here, src, slots, device, far, i):
        src[...] = row
        slots[pl.ds(here, 1)] = row.reshape(1, 1, 128)
        for k in sorted(range(1, size), key=far):
            pltpu.make_async_remote_copy(
                src_ref=src,
                dst_ref=slots.at[here],
                send_sem=red_send.at[i],
                recv_sem=red_recv.at[i],
                device_id=device(k),
                device_id_type=MESH,
            ).start()

    def collect(size, slots, i):
        most = slots.at[pl.ds(0, size - 1)]
        pltpu.make_async_copy(most, most, red_recv.at[i]).wait()
        sums = [slots[k] for k in range(size)]
        lows = sums
        while len(sums) > 1:
            odd = len(sums) % 2
            sums, lows = (
                [sums[j] + sums[j + 1] for j in range(0, len(sums) - odd, 2)] + sums[len(sums) - odd :],
                [jnp.minimum(lows[j], lows[j + 1]) for j in range(0, len(lows) - odd, 2)]
                + lows[len(lows) - odd :],
            )
        return jnp.where(lane1 == 8, lows[0], sums[0])

    def line_far(k):
        return -min(k, n_px - k)

    def plane_far(k):
        x, y = k // 2 % 4, k // 8
        return -(min(x, 4 - x) + min(y, 4 - y))

    spread_row(row, n_py, py, row_plane, got_plane, lambda k: (px, at_py(k)), plane_far, 0)
    halo[3].wait_recv()
    halo[6].start()
    halo[7].start()
    for k in range(3, rounds + 1):
        pass_on(k)
    row = collect(n_py, got_plane, 0)
    spread_row(row, n_px, px, row_line, got_line, lambda k: (at_px(k), py), line_far, 1)

    halo[6].wait_recv()
    halo[7].wait_recv()
    beyond = solve(columns_right(edges(strips_right)))
    lane6 = lax.broadcasted_iota(jnp.int32, (6, 8, 128), 2)
    mine = [jnp.where(lane6 < 123, a, b) for a, b in zip(part, beyond)]
    row = collect(n_px, got_line, 1)

    row = jnp.broadcast_to(row, (8, 128))
    splat = [jnp.broadcast_to(row[:, k : k + 1], (8, 128)) for k in range(9)]
    accel = coefficients(splat[:8])
    min_step = splat[8]
    total = accel[0] * mine[0]
    for k in range(1, ITERS):
        total = total + accel[k] * mine[k]
    out_gain[...] = min_step * total
    out_step[...] = min_step

    for copy in halo:
        copy.wait_send()
    for i, (slots, size) in enumerate(((got_plane, n_py), (got_line, n_px))):
        most = slots.at[pl.ds(0, size - 1)]
        pltpu.make_async_copy(most, most, red_send.at[i]).wait()


def local(n_px, n_py, disp, vel, force, mass, thick, added, stiff, elements, counts):
    tiles = elements.shape[0]
    vmem = lambda *dims: pltpu.VMEM(dims, F32)
    dma = lambda n: pltpu.SemaphoreType.DMA((n,))
    gain, step = pl.pallas_call(
        functools.partial(kernel, n_px, n_py),
        out_shape=[jax.ShapeDtypeStruct(disp.shape, F32), jax.ShapeDtypeStruct((8, 128), F32)],
        in_specs=[pl.BlockSpec(memory_space=pltpu.HBM)] * 7 + [pl.BlockSpec(memory_space=pltpu.SMEM)],
        out_specs=[pl.BlockSpec(memory_space=pltpu.VMEM)] * 2,
        scratch_shapes=[
            vmem(FIELDS, 8, 128),
            vmem(2, 8, 128),
            vmem(24, 24),
            pltpu.VMEM((tiles, 128), jnp.int32),
            vmem(FIELDS, 8, 128),
            vmem(FIELDS, 8, 128),
            vmem(2, 8, 128),
            vmem(3, 8, 128),
            vmem(3, 8, 128),
            vmem(1, 128),
            vmem(1, 128),
            vmem(n_py, 1, 128),
            vmem(n_px, 1, 128),
            dma(4),
            dma(8),
            dma(8),
            dma(2),
            dma(2),
            pltpu.SemaphoreType.REGULAR((6,)),
        ],
        compiler_params=pltpu.CompilerParams(
            collective_id=0, has_side_effects=True, vmem_limit_bytes=8 << 20
        ),
        name="crash_step",
    )(*(pltpu.with_memory_space_constraint(x, pltpu.HBM) for x in (disp, force, mass, thick, added, stiff, elements)), counts)
    new_velocity = vel + gain
    new_displacement = disp + step * new_velocity
    return new_velocity, new_displacement


def solution(mesh):
    field = P(None, "px", "py")
    plane = P("px", "py")
    return jax.shard_map(
        functools.partial(local, mesh.shape["px"], mesh.shape["py"]),
        mesh=mesh,
        in_specs=(field, field, field, plane, plane, plane, P(), plane, plane),
        out_specs=(field, field),
        check_vma=False,
    )
```
